256 devices in a mesh: grp: 8 (over z_hi, y), slab: 32 (over x, z_lo, core).
Axes of the slice: x: 4, y: 4, z: 8 (z_hi: 2, z_lo: 4; z = z_hi * 4 + z_lo), core: 2. Of those that a mesh axis runs over, the one named last changes fastest.
Arguments:
- orbital_alpha: bfloat16 [8, 1536, 2560], P('grp', 'slab'), may hold values from -0.4375 to 0.4375
- orbital_beta: bfloat16 [8, 1536, 2560], P('grp', 'slab'), may hold values from -0.4375 to 0.4375
- occ_alpha: float32 [8], replicated, may hold values from -2 to -0.3
- occ_beta: float32 [8], replicated, may hold values from -2 to -0.3
- virt_alpha: float32 [1536], replicated, may hold values from 0.1 to 3
- virt_beta: float32 [1536], replicated, may hold values from 0.1 to 3
Outputs:
- grad_alpha: float32 [8, 1536, 2560], P('grp', 'slab')
- grad_beta: float32 [8, 1536, 2560], P('grp', 'slab')
The draws below stay inside these ranges and needn't reach their ends.
All inputs are finite; a program needn't handle non-finite values.
Results may differ from the reference program's by a relative error of at most 0.0013.
Values may be sent and summed in bfloat16 or wider, within the bound.
A program may use at most 128 MiB of HBM per device.

```python
import jax
import jax.numpy as jnp
from jax import lax

NV = 1536
NAUX = 2560
NI = 8
NJ = 8
A_DEV = 48


def level_of(rng, extent, cuts, smallest, largest):
    def one(position, blocks):
        heights = jax.random.uniform(jax.random.fold_in(jax.random.fold_in(rng, 6), position), (blocks,), jnp.float32, smallest / len(cuts), largest / len(cuts))
        return jnp.repeat(jnp.exp(heights), extent[position] // blocks).reshape((-1,) + (1,) * (len(extent) - position - 1))

    gain = one(*cuts[0])
    for cut in cuts[1:]:
        gain = gain * one(*cut)
    return gain


def normal_values(stream_key, shape, deviation, reach, cuts=(), kind=jnp.bfloat16):
    drawn = jax.random.normal(stream_key, shape, jnp.float32) * deviation
    if len(cuts) > 0:
        drawn = level_of(stream_key, shape, cuts, -0.22, 0.18) * drawn
    return jnp.clip(drawn, min=-reach, max=reach).astype(kind)


def setup_inputs(seed: int = 0) -> dict:
    streams_of = jax.random.split(jax.random.key(seed), 7)
    orbital_alpha = normal_values(streams_of[0], (NI, NV, NAUX), (1.75 / (NI * NV) ** 0.3333), 0.4375, ((0, 8), (1, 32)))
    orbital_beta = normal_values(streams_of[1], (NJ, NV, NAUX), (1.75 / (NJ * NV) ** 0.3333), 0.4375, ((0, 8), (1, 32)))
    occ_alpha = jnp.clip(jax.random.uniform(streams_of[2], (NI,), jnp.float32, -2.0, -0.3), -2.0, -0.3)
    occ_beta = jnp.clip(jax.random.uniform(streams_of[3], (NJ,), jnp.float32, -2.0, -0.3), -2.0, -0.3)
    virt_alpha = jnp.clip(jax.random.uniform(streams_of[4], (NV,), jnp.float32, 0.1, 3.0), 0.1, 3.0)
    virt_beta = jnp.clip(jax.random.uniform(streams_of[5], (NV,), jnp.float32, 0.1, 3.0), 0.1, 3.0)
    return dict(orbital_alpha=orbital_alpha, orbital_beta=orbital_beta, occ_alpha=occ_alpha, occ_beta=occ_beta, virt_alpha=virt_alpha, virt_beta=virt_beta)


def reference(orbital_alpha, orbital_beta, occ_alpha, occ_beta, virt_alpha, virt_beta):
    slabs = NV // A_DEV
    beta_blocks = jnp.moveaxis(orbital_beta.reshape(NJ, slabs, A_DEV, NAUX), 1, 0)
    virt_blocks = virt_beta.reshape(slabs, A_DEV)
    alpha_wide = orbital_alpha.astype(jnp.float32)

    def one_slab(carried, pieces):
        panel_beta, virt_slab = pieces
        panel_wide = panel_beta.astype(jnp.float32)
        integrals = jnp.einsum('iaq,jbq->iajb', alpha_wide, panel_wide)
        denominator = virt_alpha[None, :, None, None] + virt_slab[None, None, None, :] - occ_alpha[:, None, None, None] - occ_beta[None, None, :, None]
        amplitudes = (-integrals / denominator).astype(jnp.bfloat16)
        amplitudes = lax.optimization_barrier(amplitudes).astype(jnp.float32)
        partial_value = jnp.einsum('iajb,jbq->iaq', amplitudes, panel_wide)
        carried = carried + partial_value
        beta_part = jnp.einsum('iajb,iaq->jbq', amplitudes, alpha_wide)
        return carried, beta_part

    start_sum = jnp.zeros((NI, NV, NAUX), jnp.float32)
    grad_alpha, stacked = lax.scan(one_slab, start_sum, (beta_blocks, virt_blocks))
    grad_beta = jnp.moveaxis(stacked, 0, 1).reshape(NJ, NV, NAUX)
    return grad_alpha, grad_beta
```

```python
import functools

import jax
import jax.numpy as jnp
from jax import lax
from jax.experimental import pallas as pl
from jax.experimental.pallas import tpu as pltpu
from jax.sharding import PartitionSpec as P

MESH = pl.DeviceIdType.MESH
ROWS = 48
HALF = 1280
QUART = 640
BROWS = 768
POS = {0: 0, 1: 1, 7: 2, 2: 3, 6: 4, 3: 5, 5: 6, 4: 7}
SCALE = 512.0
TINY = 1e-37
F32 = jnp.float32
BF16 = jnp.bfloat16


def encode(value):
    scaled = value * SCALE
    square = scaled * jnp.abs(scaled)
    return (square * jnp.abs(square)).astype(BF16)


def decode(code):
    wide = code.astype(F32)
    size = jnp.abs(wide)
    root = lax.rsqrt(lax.rsqrt(jnp.maximum(size, TINY))) * (1.0 / SCALE)
    root = jnp.where(size > TINY, root, 0.0)
    return jnp.where(wide < 0.0, -root, root)


def kernel(
    occ_a, occ_b, virt_a, virt_b, a_hbm, b_hbm, ga_out, gb_out,
    A, B, I, T, TT, G, GBO, GBS, GBR, S1, R1A, R1B, S2, R2A, R2B, SZ, RZ, RZ0, VA,
    local_sem, send_sem, recv_sem,
):
    grp = lax.axis_index("grp")
    slab = lax.axis_index("slab")
    z_hi, y = grp // 4, grp % 4
    x, z_lo, core = slab // 8, (slab // 2) % 4, slab % 2
    z = z_hi * 4 + z_lo

    def device(dx=0, dy=0, dz=0, dc=0):
        nx, ny, nz, nc = (x + dx) % 4, (y + dy) % 4, (z + dz) % 8, (core + dc) % 2
        return ((nz // 4) * 4 + ny, nx * 8 + (nz % 4) * 2 + nc)

    xy = {(0, 1): device(dx=1), (0, -1): device(dx=3), (1, 1): device(dy=1), (1, -1): device(dy=3)}
    zdev = {1: device(dz=1), -1: device(dz=7)}
    sibling = device(dc=1)

    local = []
    for h in range(2):
        cols = pl.ds(h * HALF, HALF)
        local.append(pltpu.make_async_copy(a_hbm.at[0, :, cols], A.at[h, 0, 0], local_sem.at[h]))
        local.append(pltpu.make_async_copy(b_hbm.at[0, :, cols], B.at[h, pl.ds(0, ROWS)], local_sem.at[2 + h]))
    for copy in local:
        copy.start()

    barrier = pltpu.get_barrier_semaphore()
    for neighbour in list(xy.values()) + list(zdev.values()) + [sibling]:
        pl.semaphore_signal(barrier, inc=1, device_id=neighbour, device_id_type=MESH)

    eye = lax.broadcasted_iota(jnp.int32, (ROWS, ROWS), 0) == lax.broadcasted_iota(jnp.int32, (ROWS, ROWS), 1)
    for dx in range(4):
        row = virt_a[pl.ds(((x + dx) % 4) * 8 + z_lo * 2 + core, 1), :]
        column = jnp.sum(jnp.where(eye, jnp.broadcast_to(row, (ROWS, ROWS)), 0.0), axis=1, keepdims=True)
        VA[dx] = jnp.broadcast_to(column, (ROWS, 128))
    lanes = lax.broadcasted_iota(jnp.int32, (8, BROWS), 1)
    part = virt_b[pl.ds(x, 1), :]
    ring_virt = jnp.broadcast_to(jnp.concatenate([part, part], axis=1), (8, BROWS))
    ring_occ = jnp.where(lanes < 384, occ_b[y], occ_b[4 + y])
    vb = jnp.zeros((8, BROWS), F32)
    ob = jnp.zeros((8, BROWS), F32)
    for r, p in POS.items():
        there = (z + r) % 8
        for k in range(2):
            shift = (96 * p + 768 - 96 * there + (48 * core if k else 768 - 48 * core)) % 768
            here = (lanes >= 96 * p + 48 * k) & (lanes < 96 * p + 48 * k + 48)
            vb = jnp.where(here, pltpu.roll(ring_virt, shift, 1), vb)
            ob = jnp.where(here, pltpu.roll(ring_occ, shift, 1), ob)
    vb, ob = vb[0:1], ob[0:1]

    copies = {}

    def remote(name, src, dst, dev):
        index = len(copies)
        copies[name] = pltpu.make_async_remote_copy(
            src_ref=src, dst_ref=dst, send_sem=send_sem.at[index], recv_sem=recv_sem.at[index],
            device_id=dev, device_id_type=MESH,
        )

    def start(*names):
        for name in names:
            copies[name].start()

    def arrived(*names):
        for name in names:
            copies[name].wait_recv()

    def ablock(h, d1, d2):
        return A.at[0, d2, d1] if h == 0 else A.at[1, d1, d2]

    def bblock(h, r, k=0):
        return B.at[h, pl.ds(POS[r % 8] * 96 + k * ROWS, ROWS)]

    first, second = pl.ds(0, QUART), pl.ds(QUART, QUART)
    for h in range(2):
        one, two = h, 1 - h
        remote(("p1+", h), ablock(h, 0, 0), ablock(h, 3, 0), xy[one, 1])
        remote(("p1-", h), ablock(h, 0, 0), ablock(h, 1, 0), xy[one, -1])
        remote(("p1f+", h), ablock(h, 3, 0).at[:, first], ablock(h, 2, 0).at[:, first], xy[one, 1])
        remote(("p1f-", h), ablock(h, 1, 0).at[:, second], ablock(h, 2, 0).at[:, second], xy[one, -1])
        for u in range(4):
            remote(("p2+", h, u), ablock(h, u, 0), ablock(h, u, 3), xy[two, 1])
            remote(("p2-", h, u), ablock(h, u, 0), ablock(h, u, 1), xy[two, -1])
            if u % 2 == 0:
                remote(("p2f", h, u), ablock(h, u, 3), ablock(h, u, 2), xy[two, 1])
            else:
                remote(("p2f", h, u), ablock(h, u, 1), ablock(h, u, 2), xy[two, -1])
        for k in range(1, 4):
            remote(("z+", h, k), bblock(h, 1 - k), bblock(h, -k), zdev[1])
            remote(("z-", h, k), bblock(h, k - 1), bblock(h, k), zdev[-1])
        if h == 0:
            remote(("z4", h), bblock(h, 5), bblock(h, 4), zdev[1])
        else:
            remote(("z4", h), bblock(h, 3), bblock(h, 4), zdev[-1])
        for r in range(8):
            remote(("sib", h, r), bblock(h, r, 0), bblock(h, r, 1), sibling)

        for u in range(4):
            remote(("1a", h, u), S1.at[h, 2, u], R1A.at[h, u], xy[two, 1 if u % 2 == 0 else -1])
            remote(("1b+", h, u), S1.at[h, 1, u], R1B.at[h, 0, u], xy[two, 1])
            remote(("1b-", h, u), S1.at[h, 3, u], R1B.at[h, 1, u], xy[two, -1])
        remote(("2a+", h), S2.at[h, 2, :, first], R2A.at[h, :, first], xy[one, 1])
        remote(("2a-", h), S2.at[h, 2, :, second], R2A.at[h, :, second], xy[one, -1])
        remote(("2b+", h), S2.at[h, 1], R2B.at[h, 0], xy[one, 1])
        remote(("2b-", h), S2.at[h, 3], R2B.at[h, 1], xy[one, -1])
        if h == 0:
            remote(("rz", h, 4), SZ.at[h, 4], RZ.at[h, 3], zdev[1])
        else:
            remote(("rz", h, 4), SZ.at[h, 4], RZ.at[h, 5], zdev[-1])
        for r in (3, 2):
            remote(("rz", h, r), SZ.at[h, r], RZ.at[h, r - 1], zdev[1])
            remote(("rz", h, 8 - r), SZ.at[h, 8 - r], RZ.at[h, 9 - r], zdev[-1])
        remote(("rz", h, 1), SZ.at[h, 1], RZ0.at[h, 0], zdev[1])
        remote(("rz", h, 7), SZ.at[h, 7], RZ0.at[h, 1], zdev[-1])
        for p in range(8):
            remote(("gsib", h, p), GBS.at[h, p], GBR.at[h, p], sibling)

    def integrals(h, d2, j):
        left = (A[0, d2] if h == 0 else A[1, :, d2]).reshape(4 * ROWS, HALF)
        right = B[h, pl.ds(j * 256, 256), :]
        value = lax.dot_general(left, right, (((1,), (1,)), ((), ())), preferred_element_type=F32)
        value = value.reshape(4, ROWS, 256)
        if h == 0:
            I[0, d2, :, :, pl.ds(j * 256, 256)] = value
        else:
            I[1, :, d2, :, pl.ds(j * 256, 256)] = value

    def amplitudes(low, high):
        def one(block, carry):
            dy, dx = block // 4, block % 4
            occ = occ_a[z_hi * 4 + (y + dy) % 4]
            for tile in range(low, high):
                at = pl.ds(tile * 128, 128)
                number = I[0, dy, dx, :, at] + I[1, dy, dx, :, at]
                below = VA[dx] + vb[:, tile * 128:tile * 128 + 128] - occ - ob[:, tile * 128:tile * 128 + 128]
                T[dy, dx, :, at] = (-number / below).astype(BF16)
            return carry

        lax.fori_loop(0, 16, one, 0)
        for tile in range(low, high):
            square = T[:, :, :, pl.ds(tile * 128, 128)].reshape(BROWS, 128)
            TT[pl.ds(tile * 128, 128), :] = jnp.transpose(square.astype(F32)).astype(BF16)

    def alpha_term(h, d2):
        raw = {2: (0, 1, 2, 3), 1: (1, 3), 3: (0, 2), 0: ()}[d2]

        def one(j, carry):
            at = pl.ds(pl.multiple_of(j * 256, 256), 256)
            left = (T[d2] if h == 0 else T[:, d2]).reshape(4 * ROWS, BROWS)
            value = jnp.dot(left, B[h, :, at], preferred_element_type=F32)
            for u in range(4):
                block = value[u * ROWS:(u + 1) * ROWS]
                if u in raw:
                    S1[h, d2, u, :, at] = encode(block)
                else:
                    G[h, d2, u, :, at] = block
            return carry

        lax.fori_loop(0, 5, one, 0)

    def beta_term(h, low, high):
        def one(j, carry):
            at = pl.ds(pl.multiple_of(j * 256, 256), 256)
            right = A[h, :, :, :, at].reshape(BROWS, 256)
            value = jnp.dot(TT[pl.ds(low * 96, (high - low) * 96), :], right, preferred_element_type=F32)
            for p in range(low, high):
                base = (p - low) * 96
                GBO[h, p, :, at] = value[base:base + ROWS]
                GBS[h, p, :, at] = value[base + ROWS:base + 2 * ROWS]
            return carry

        lax.fori_loop(0, 5, one, 0)
        for p in range(low, high):
            start(("gsib", h, p))

    def by_rows(body):
        def one(step, carry):
            body(pl.ds(pl.multiple_of(step * 16, 16), 16))
            return carry

        lax.fori_loop(0, ROWS // 16, one, 0)

    for copy in local:
        copy.wait()
    pl.semaphore_wait(barrier, 7)
    H = (0, 1)
    for h in H:
        start(("p1+", h), ("p1-", h))
    for h in H:
        start(("z+", h, 1), ("z-", h, 1))
    for h in H:
        start(("p2+", h, 0), ("p2-", h, 0))
    for h in H:
        start(("sib", h, 0))
    for h in H:
        arrived(("p1+", h), ("p1-", h))
        start(("p1f+", h), ("p1f-", h))
    for u in (3, 1):
        for h in H:
            start(("p2+", h, u), ("p2-", h, u))
    for h in H:
        arrived(("z+", h, 1), ("z-", h, 1))
        start(("z+", h, 2), ("z-", h, 2), ("sib", h, 1), ("sib", h, 7))
    for h in H:
        arrived(("p1f+", h), ("p1f-", h))
        start(("p2+", h, 2), ("p2-", h, 2))
    for h in H:
        arrived(("p2+", h, 0), ("p2-", h, 0))
        start(("p2f", h, 0))
    for h in H:
        arrived(("sib", h, 0), ("sib", h, 1), ("sib", h, 7))
        integrals(h, 0, 0)
    for h in H:
        arrived(("z+", h, 2), ("z-", h, 2))
        start(("z+", h, 3), ("z-", h, 3), ("sib", h, 2), ("sib", h, 6))
    for u in (3, 1):
        for h in H:
            arrived(("p2+", h, u), ("p2-", h, u))
            start(("p2f", h, u))
    for h in H:
        arrived(("p2+", h, 2), ("p2-", h, 2))
        start(("p2f", h, 2))
    for h in H:
        integrals(h, 1, 0)
        integrals(h, 3, 0)
    for h in H:
        arrived(("z+", h, 3), ("z-", h, 3))
        start(("z4", h), ("sib", h, 3), ("sib", h, 5))
    for h in H:
        arrived(("sib", h, 2), ("sib", h, 6), ("sib", h, 3))
        for d2 in (0, 1, 3):
            integrals(h, d2, 1)
    for h in H:
        for u in (0, 3, 1, 2):
            arrived(("p2f", h, u))
        integrals(h, 2, 0)
        integrals(h, 2, 1)
    for h in H:
        arrived(("z4", h))
        start(("sib", h, 4))
    amplitudes(0, 4)
    for h in H:
        arrived(("sib", h, 5), ("sib", h, 4))
        for d2 in range(4):
            integrals(h, d2, 2)
    amplitudes(4, 6)

    def add_first(h, u):
        d2 = 1 if u % 2 == 0 else 3
        arrived(("1a", h, u))

        def body(rows):
            S1[h, d2, u, rows] = encode(G[h, d2, u, rows] + decode(R1A[h, u, rows]))

        by_rows(body)
        start(("1b+" if d2 == 1 else "1b-", h, u))

    def plane_sum(h, u, rows):
        return G[h, 0, u, rows] + decode(R1B[h, 0, u, rows]) + decode(R1B[h, 1, u, rows])

    def z_send(h, r):
        p = POS[r]
        chained = r in (1, 2, 6, 7) or (r, h) in ((3, 0), (5, 1))
        arrived(("gsib", h, p))
        if r == 3 and h == 0 or r == 5 and h == 1:
            arrived(("rz", h, 4))
        elif chained:
            arrived(("rz", h, r + 1 if r < 4 else r - 1))

        def body(rows):
            value = GBO[h, p, rows] + GBR[h, p, rows]
            if chained:
                value = value + decode(RZ[h, r, rows])
            SZ[h, r, rows] = encode(value)

        by_rows(body)
        start(("rz", h, r))

    order = (2, 1, 3, 0)
    for h in H:
        alpha_term(h, 2)
        for u in order:
            start(("1a", h, u))
    for h in H:
        beta_term(h, 7, 8)
    for h in H:
        alpha_term(h, 1)
        start(("1b+", h, 1), ("1b+", h, 3))
    for h in H:
        z_send(h, 4)
    for h in H:
        alpha_term(h, 3)
        start(("1b-", h, 2), ("1b-", h, 0))
    for h in H:
        beta_term(h, 5, 7)
    z_send(1, 3)
    z_send(0, 5)
    for h in H:
        add_first(h, 2)
    z_send(0, 3)
    z_send(1, 5)
    for u in (1, 3, 0):
        for h in H:
            add_first(h, u)
    for h in H:
        beta_term(h, 3, 5)
    for h in H:
        alpha_term(h, 0)
    for h in H:
        z_send(h, 2)
        z_send(h, 6)
    for h in H:
        beta_term(h, 1, 3)
    for h in H:
        beta_term(h, 0, 1)

    for h in H:
        arrived(("1b+", h, 2), ("1b-", h, 2))

        def body(rows):
            S2[h, 2, rows] = encode(plane_sum(h, 2, rows))

        by_rows(body)
        start(("2a+", h), ("2a-", h))
    for h in H:
        z_send(h, 1)
        z_send(h, 7)
    for h in H:
        for u in (1, 3):
            arrived(("1b+", h, u), ("1b-", h, u))

            def body(rows):
                G[h, 0, u, rows] = plane_sum(h, u, rows)

            by_rows(body)
    for h in H:
        for u in (1, 3):
            arrived(("2a+" if u == 1 else "2a-", h))
            added, plain = (first, second) if u == 1 else (second, first)

            def body(rows):
                S2[h, u, rows, added] = encode(G[h, 0, u, rows, added] + decode(R2A[h, rows, added]))
                S2[h, u, rows, plain] = encode(G[h, 0, u, rows, plain])

            by_rows(body)
            start(("2b+" if u == 1 else "2b-", h))
    for h in H:
        arrived(("1b+", h, 0), ("1b-", h, 0))

        def body(rows):
            G[h, 0, 0, rows] = plane_sum(h, 0, rows)

        by_rows(body)
    for h in H:
        arrived(("gsib", h, 0), ("rz", h, 1), ("rz", h, 7))

        def body(rows):
            gb_out[0, rows, pl.ds(h * HALF, HALF)] = (
                GBO[h, 0, rows] + GBR[h, 0, rows] + decode(RZ0[h, 0, rows]) + decode(RZ0[h, 1, rows])
            )

        by_rows(body)
    for h in H:
        arrived(("2b+", h), ("2b-", h))

        def body(rows):
            ga_out[0, rows, pl.ds(h * HALF, HALF)] = (
                G[h, 0, 0, rows] + decode(R2B[h, 0, rows]) + decode(R2B[h, 1, rows])
            )

        by_rows(body)
    for copy in copies.values():
        copy.wait_send()


def body(orbital_alpha, orbital_beta, occ_alpha, occ_beta, virt_alpha, virt_beta):
    block = (ROWS, HALF)
    smem = pl.BlockSpec(memory_space=pltpu.SMEM)
    vmem = pl.BlockSpec(memory_space=pltpu.VMEM)
    hbm = pl.BlockSpec(memory_space=pl.ANY)
    out = jax.ShapeDtypeStruct((1, ROWS, 2 * HALF), F32)
    count = 128
    return pl.pallas_call(
        kernel,
        out_shape=(out, out),
        in_specs=[smem, smem, vmem, vmem, hbm, hbm],
        out_specs=(vmem, vmem),
        scratch_shapes=[
            pltpu.VMEM((2, 4, 4) + block, BF16),
            pltpu.VMEM((2, BROWS, HALF), BF16),
            pltpu.VMEM((2, 4, 4, ROWS, BROWS), F32),
            pltpu.VMEM((4, 4, ROWS, BROWS), BF16),
            pltpu.VMEM((BROWS, BROWS), BF16),
            pltpu.VMEM((2, 4, 4) + block, F32),
            pltpu.VMEM((2, 8) + block, F32),
            pltpu.VMEM((2, 8) + block, F32),
            pltpu.VMEM((2, 8) + block, F32),
            pltpu.VMEM((2, 4, 4) + block, BF16),
            pltpu.VMEM((2, 4) + block, BF16),
            pltpu.VMEM((2, 2, 4) + block, BF16),
            pltpu.VMEM((2, 4) + block, BF16),
            pltpu.VMEM((2,) + block, BF16),
            pltpu.VMEM((2, 2) + block, BF16),
            pltpu.VMEM((2, 8) + block, BF16),
            pltpu.VMEM((2, 8) + block, BF16),
            pltpu.VMEM((2, 2) + block, BF16),
            pltpu.VMEM((4, ROWS, 128), F32),
            pltpu.SemaphoreType.DMA((4,)),
            pltpu.SemaphoreType.DMA((count,)),
            pltpu.SemaphoreType.DMA((count,)),
        ],
        compiler_params=pltpu.CompilerParams(
            collective_id=0, has_side_effects=True, vmem_limit_bytes=66 * 1000 * 1000
        ),
    )(occ_alpha, occ_beta, virt_alpha.reshape(32, ROWS), virt_beta.reshape(4, 384), orbital_alpha, orbital_beta)


def solution(mesh):
    in_specs = (P("grp", "slab", None), P("grp", "slab", None), P(), P(), P(), P())
    out_specs = (P("grp", "slab", None), P("grp", "slab", None))
    return jax.shard_map(body, mesh=mesh, in_specs=in_specs, out_specs=out_specs, check_vma=False)
```

```python
import functools

import jax
import jax.numpy as jnp
from jax import lax
from jax.experimental import pallas as pl
from jax.experimental.pallas import tpu as pltpu
from jax.sharding import PartitionSpec as P

MESH = pl.DeviceIdType.MESH
ROWS = 48
HALF = 1280
QUART = 640
BROWS = 768
POS = {0: 0, 1: 1, 7: 2, 2: 3, 6: 4, 3: 5, 5: 6, 4: 7}
SCALE = 512.0
TINY = 1e-37
F32 = jnp.float32
BF16 = jnp.bfloat16


def encode(value):
    scaled = value * SCALE
    square = scaled * jnp.abs(scaled)
    return (square * jnp.abs(square)).astype(BF16)


def decode(code):
    wide = code.astype(F32)
    size = jnp.abs(wide)
    root = lax.rsqrt(lax.rsqrt(jnp.maximum(size, TINY))) * (1.0 / SCALE)
    root = jnp.where(size > TINY, root, 0.0)
    return jnp.where(wide < 0.0, -root, root)


def kernel(
    occ_a, occ_b, virt_a, virt_b, a_hbm, b_hbm, ga_out, gb_out,
    A, B, I, T, TT, G, GBO, GBS, GBR, S1, R1A, R1B, S2, R2A, R2B, SZ, RZ, RZ0, VA,
    local_sem, send_sem, recv_sem,
):
    grp = lax.axis_index("grp")
    slab = lax.axis_index("slab")
    z_hi, y = grp // 4, grp % 4
    x, z_lo, core = slab // 8, (slab // 2) % 4, slab % 2
    z = z_hi * 4 + z_lo

    def device(dx=0, dy=0, dz=0, dc=0):
        nx, ny, nz, nc = (x + dx) % 4, (y + dy) % 4, (z + dz) % 8, (core + dc) % 2
        return ((nz // 4) * 4 + ny, nx * 8 + (nz % 4) * 2 + nc)

    xy = {(0, 1): device(dx=1), (0, -1): device(dx=3), (1, 1): device(dy=1), (1, -1): device(dy=3)}
    zdev = {1: device(dz=1), -1: device(dz=7)}
    sibling = device(dc=1)

    local = []
    for h in range(2):
        cols = pl.ds(h * HALF, HALF)
        local.append(pltpu.make_async_copy(a_hbm.at[0, :, cols], A.at[h, 0, 0], local_sem.at[h]))
        local.append(pltpu.make_async_copy(b_hbm.at[0, :, cols], B.at[h, pl.ds(0, ROWS)], local_sem.at[2 + h]))
    for copy in local:
        copy.start()

    barrier = pltpu.get_barrier_semaphore()
    for neighbour in list(xy.values()) + list(zdev.values()) + [sibling]:
        pl.semaphore_signal(barrier, inc=1, device_id=neighbour, device_id_type=MESH)

    eye = lax.broadcasted_iota(jnp.int32, (ROWS, 128), 0) == lax.broadcasted_iota(jnp.int32, (ROWS, 128), 1)

    def energies(ref, column):
        return jnp.concatenate([ref[pl.ds(3 * column + i, 1), :] for i in range(3)], axis=1)

    for dx in range(4):
        row = jnp.broadcast_to(energies(virt_a, (x + dx) % 4), (8, 384))
        row = pltpu.roll(row, (384 - 96 * z_lo - 48 * core) % 384, 1)[0:1, :128]
        column = jnp.sum(jnp.where(eye, jnp.broadcast_to(row, (ROWS, 128)), 0.0), axis=1, keepdims=True)
        VA[dx] = jnp.broadcast_to(column, (ROWS, 128))
    lanes = lax.broadcasted_iota(jnp.int32, (8, BROWS), 1)
    part = energies(virt_b, x)
    ring_virt = jnp.broadcast_to(jnp.concatenate([part, part], axis=1), (8, BROWS))
    ring_occ = jnp.where(lanes < 384, occ_b[y], occ_b[4 + y])
    vb = jnp.zeros((8, BROWS), F32)
    ob = jnp.zeros((8, BROWS), F32)
    for r, p in POS.items():
        there = (z + r) % 8
        for k in range(2):
            shift = (96 * p + 768 - 96 * there + (48 * core if k else 768 - 48 * core)) % 768
            here = (lanes >= 96 * p + 48 * k) & (lanes < 96 * p + 48 * k + 48)
            vb = jnp.where(here, pltpu.roll(ring_virt, shift, 1), vb)
            ob = jnp.where(here, pltpu.roll(ring_occ, shift, 1), ob)
    vb, ob = vb[0:1], ob[0:1]

    copies = {}

    def remote(name, src, dst, dev):
        index = len(copies)
        copies[name] = pltpu.make_async_remote_copy(
            src_ref=src, dst_ref=dst, send_sem=send_sem.at[index], recv_sem=recv_sem.at[index],
            device_id=dev, device_id_type=MESH,
        )

    def start(*names):
        for name in names:
            copies[name].start()

    def arrived(*names):
        for name in names:
            copies[name].wait_recv()

    def ablock(h, d1, d2):
        return A.at[0, d2, d1] if h == 0 else A.at[1, d1, d2]

    def bblock(h, r, k=0):
        return B.at[h, pl.ds(POS[r % 8] * 96 + k * ROWS, ROWS)]

    first, second = pl.ds(0, QUART), pl.ds(QUART, QUART)
    for h in range(2):
        one, two = h, 1 - h
        remote(("p1+", h), ablock(h, 0, 0), ablock(h, 3, 0), xy[one, 1])
        remote(("p1-", h), ablock(h, 0, 0), ablock(h, 1, 0), xy[one, -1])
        remote(("p1f+", h), ablock(h, 3, 0).at[:, first], ablock(h, 2, 0).at[:, first], xy[one, 1])
        remote(("p1f-", h), ablock(h, 1, 0).at[:, second], ablock(h, 2, 0).at[:, second], xy[one, -1])
        for u in range(4):
            remote(("p2+", h, u), ablock(h, u, 0), ablock(h, u, 3), xy[two, 1])
            remote(("p2-", h, u), ablock(h, u, 0), ablock(h, u, 1), xy[two, -1])
            if u % 2 == 0:
                remote(("p2f", h, u), ablock(h, u, 3), ablock(h, u, 2), xy[two, 1])
            else:
                remote(("p2f", h, u), ablock(h, u, 1), ablock(h, u, 2), xy[two, -1])
        for k in range(1, 4):
            remote(("z+", h, k), bblock(h, 1 - k), bblock(h, -k), zdev[1])
            remote(("z-", h, k), bblock(h, k - 1), bblock(h, k), zdev[-1])
        if h == 0:
            remote(("z4", h), bblock(h, 5), bblock(h, 4), zdev[1])
        else:
            remote(("z4", h), bblock(h, 3), bblock(h, 4), zdev[-1])
        for r in range(8):
            remote(("sib", h, r), bblock(h, r, 0), bblock(h, r, 1), sibling)

        for u in range(4):
            remote(("1a", h, u), S1.at[h, 2, u], R1A.at[h, u], xy[two, 1 if u % 2 == 0 else -1])
            remote(("1b+", h, u), S1.at[h, 1, u], R1B.at[h, 0, u], xy[two, 1])
            remote(("1b-", h, u), S1.at[h, 3, u], R1B.at[h, 1, u], xy[two, -1])
        remote(("2a+", h), S2.at[h, 2, :, first], R2A.at[h, :, first], xy[one, 1])
        remote(("2a-", h), S2.at[h, 2, :, second], R2A.at[h, :, second], xy[one, -1])
        remote(("2b+", h), S2.at[h, 1], R2B.at[h, 0], xy[one, 1])
        remote(("2b-", h), S2.at[h, 3], R2B.at[h, 1], xy[one, -1])
        if h == 0:
            remote(("rz", h, 4), SZ.at[h, 4], RZ.at[h, 3], zdev[1])
        else:
            remote(("rz", h, 4), SZ.at[h, 4], RZ.at[h, 5], zdev[-1])
        for r in (3, 2):
            remote(("rz", h, r), SZ.at[h, r], RZ.at[h, r - 1], zdev[1])
            remote(("rz", h, 8 - r), SZ.at[h, 8 - r], RZ.at[h, 9 - r], zdev[-1])
        remote(("rz", h, 1), SZ.at[h, 1], RZ0.at[h, 0], zdev[1])
        remote(("rz", h, 7), SZ.at[h, 7], RZ0.at[h, 1], zdev[-1])
        for p in range(8):
            remote(("gsib", h, p), GBS.at[h, p], GBR.at[h, p], sibling)

    def integrals(h, d2, j):
        left = (A[0, d2] if h == 0 else A[1, :, d2]).reshape(4 * ROWS, HALF)
        right = B[h, pl.ds(j * 256, 256), :]
        value = lax.dot_general(left, right, (((1,), (1,)), ((), ())), preferred_element_type=F32)
        value = value.reshape(4, ROWS, 256)
        if h == 0:
            I[0, d2, :, :, pl.ds(j * 256, 256)] = value
        else:
            I[1, :, d2, :, pl.ds(j * 256, 256)] = value

    def amplitudes(low, high):
        def one(block, carry):
            dy, dx = block // 4, block % 4
            occ = occ_a[z_hi * 4 + (y + dy) % 4]
            for tile in range(low, high):
                at = pl.ds(tile * 128, 128)
                number = I[0, dy, dx, :, at] + I[1, dy, dx, :, at]
                below = VA[dx] + vb[:, tile * 128:tile * 128 + 128] - occ - ob[:, tile * 128:tile * 128 + 128]
                T[dy, dx, :, at] = (-number / below).astype(BF16)
            return carry

        lax.fori_loop(0, 16, one, 0)
        for tile in range(low, high):
            square = T[:, :, :, pl.ds(tile * 128, 128)].reshape(BROWS, 128)
            TT[pl.ds(tile * 128, 128), :] = jnp.transpose(square.astype(F32)).astype(BF16)

    def alpha_term(h, d2):
        raw = {2: (0, 1, 2, 3), 1: (1, 3), 3: (0, 2), 0: ()}[d2]

        def one(j, carry):
            at = pl.ds(pl.multiple_of(j * 256, 256), 256)
            left = (T[d2] if h == 0 else T[:, d2]).reshape(4 * ROWS, BROWS)
            value = jnp.dot(left, B[h, :, at], preferred_element_type=F32)
            for u in range(4):
                block = value[u * ROWS:(u + 1) * ROWS]
                if u in raw:
                    S1[h, d2, u, :, at] = encode(block)
                else:
                    G[h, d2, u, :, at] = block
            return carry

        lax.fori_loop(0, 5, one, 0, unroll=True)

    def beta_term(h, low, high):
        def one(j, carry):
            at = pl.ds(pl.multiple_of(j * 256, 256), 256)
            right = A[h, :, :, :, at].reshape(BROWS, 256)
            value = jnp.dot(TT[pl.ds(low * 96, (high - low) * 96), :], right, preferred_element_type=F32)
            for p in range(low, high):
                base = (p - low) * 96
                GBO[h, p, :, at] = value[base:base + ROWS]
                GBS[h, p, :, at] = value[base + ROWS:base + 2 * ROWS]
            return carry

        lax.fori_loop(0, 5, one, 0, unroll=True)
        for p in range(low, high):
            start(("gsib", h, p))

    def by_rows(body):
        def one(step, carry):
            body(pl.ds(pl.multiple_of(step * 16, 16), 16))
            return carry

        lax.fori_loop(0, ROWS // 16, one, 0)

    for copy in local:
        copy.wait()
    pl.semaphore_wait(barrier, 7)
    H = (0, 1)
    for h in H:
        start(("p1+", h), ("p1-", h))
    for h in H:
        start(("z+", h, 1), ("z-", h, 1))
    for h in H:
        start(("p2+", h, 0), ("p2-", h, 0))
    for h in H:
        start(("sib", h, 0))
    for h in H:
        arrived(("p1+", h), ("p1-", h))
        start(("p1f+", h), ("p1f-", h))
    for u in (3, 1):
        for h in H:
            start(("p2+", h, u), ("p2-", h, u))
    for h in H:
        arrived(("z+", h, 1), ("z-", h, 1))
        start(("z+", h, 2), ("z-", h, 2), ("sib", h, 1), ("sib", h, 7))
    for h in H:
        arrived(("p1f+", h), ("p1f-", h))
        start(("p2+", h, 2), ("p2-", h, 2))
    for h in H:
        arrived(("p2+", h, 0), ("p2-", h, 0))
        start(("p2f", h, 0))
    for h in H:
        arrived(("sib", h, 0), ("sib", h, 1), ("sib", h, 7))
        integrals(h, 0, 0)
    for h in H:
        arrived(("z+", h, 2), ("z-", h, 2))
        start(("z+", h, 3), ("z-", h, 3), ("sib", h, 2), ("sib", h, 6))
    for u in (3, 1):
        for h in H:
            arrived(("p2+", h, u), ("p2-", h, u))
            start(("p2f", h, u))
    for h in H:
        arrived(("p2+", h, 2), ("p2-", h, 2))
        start(("p2f", h, 2))
    for h in H:
        integrals(h, 1, 0)
        integrals(h, 3, 0)
    for h in H:
        arrived(("z+", h, 3), ("z-", h, 3))
        start(("z4", h), ("sib", h, 3), ("sib", h, 5))
    for h in H:
        arrived(("sib", h, 2), ("sib", h, 6), ("sib", h, 3))
        for d2 in (0, 1, 3):
            integrals(h, d2, 1)
    for h in H:
        for u in (0, 3, 1, 2):
            arrived(("p2f", h, u))
        integrals(h, 2, 0)
        integrals(h, 2, 1)
    for h in H:
        arrived(("z4", h))
        start(("sib", h, 4))
    amplitudes(0, 4)
    for h in H:
        arrived(("sib", h, 5), ("sib", h, 4))
        for d2 in range(4):
            integrals(h, d2, 2)
    amplitudes(4, 6)

    def add_first(h, u):
        d2 = 1 if u % 2 == 0 else 3
        arrived(("1a", h, u))

        def body(rows):
            S1[h, d2, u, rows] = encode(G[h, d2, u, rows] + decode(R1A[h, u, rows]))

        by_rows(body)
        start(("1b+" if d2 == 1 else "1b-", h, u))

    def plane_sum(h, u, rows):
        return G[h, 0, u, rows] + decode(R1B[h, 0, u, rows]) + decode(R1B[h, 1, u, rows])

    def z_send(h, r):
        p = POS[r]
        chained = r in (1, 2, 6, 7) or (r, h) in ((3, 0), (5, 1))
        arrived(("gsib", h, p))
        if r == 3 and h == 0 or r == 5 and h == 1:
            arrived(("rz", h, 4))
        elif chained:
            arrived(("rz", h, r + 1 if r < 4 else r - 1))

        def body(rows):
            value = GBO[h, p, rows] + GBR[h, p, rows]
            if chained:
                value = value + decode(RZ[h, r, rows])
            SZ[h, r, rows] = encode(value)

        by_rows(body)
        start(("rz", h, r))

    order = (2, 1, 3, 0)
    for h in H:
        alpha_term(h, 2)
        for u in order:
            start(("1a", h, u))
    for h in H:
        beta_term(h, 7, 8)
    for h in H:
        alpha_term(h, 1)
        start(("1b+", h, 1), ("1b+", h, 3))
    for h in H:
        z_send(h, 4)
    for h in H:
        alpha_term(h, 3)
        start(("1b-", h, 2), ("1b-", h, 0))
    for h in H:
        beta_term(h, 5, 7)
    z_send(1, 3)
    z_send(0, 5)
    for h in H:
        add_first(h, 2)
    z_send(0, 3)
    z_send(1, 5)
    for u in (1, 3, 0):
        for h in H:
            add_first(h, u)
    for h in H:
        beta_term(h, 3, 5)
    for h in H:
        alpha_term(h, 0)
    for h in H:
        z_send(h, 2)
        z_send(h, 6)
    for h in H:
        beta_term(h, 1, 3)
    for h in H:
        beta_term(h, 0, 1)

    for h in H:
        arrived(("1b+", h, 2), ("1b-", h, 2))

        def body(rows):
            S2[h, 2, rows] = encode(plane_sum(h, 2, rows))

        by_rows(body)
        start(("2a+", h), ("2a-", h))
    for h in H:
        z_send(h, 1)
        z_send(h, 7)
    for h in H:
        for u in (1, 3):
            arrived(("1b+", h, u), ("1b-", h, u))

            def body(rows):
                G[h, 0, u, rows] = plane_sum(h, u, rows)

            by_rows(body)
    for h in H:
        for u in (1, 3):
            arrived(("2a+" if u == 1 else "2a-", h))
            added, plain = (first, second) if u == 1 else (second, first)

            def body(rows):
                S2[h, u, rows, added] = encode(G[h, 0, u, rows, added] + decode(R2A[h, rows, added]))
                S2[h, u, rows, plain] = encode(G[h, 0, u, rows, plain])

            by_rows(body)
            start(("2b+" if u == 1 else "2b-", h))
    for h in H:
        arrived(("1b+", h, 0), ("1b-", h, 0))

        def body(rows):
            G[h, 0, 0, rows] = plane_sum(h, 0, rows)

        by_rows(body)
    for h in H:
        arrived(("gsib", h, 0), ("rz", h, 1), ("rz", h, 7))

        def body(rows):
            gb_out[0, rows, pl.ds(h * HALF, HALF)] = (
                GBO[h, 0, rows] + GBR[h, 0, rows] + decode(RZ0[h, 0, rows]) + decode(RZ0[h, 1, rows])
            )

        by_rows(body)
    for h in H:
        arrived(("2b+", h), ("2b-", h))

        def body(rows):
            ga_out[0, rows, pl.ds(h * HALF, HALF)] = (
                G[h, 0, 0, rows] + decode(R2B[h, 0, rows]) + decode(R2B[h, 1, rows])
            )

        by_rows(body)
    for copy in copies.values():
        copy.wait_send()


def body(orbital_alpha, orbital_beta, occ_alpha, occ_beta, virt_alpha, virt_beta):
    block = (ROWS, HALF)
    smem = pl.BlockSpec(memory_space=pltpu.SMEM)
    vmem = pl.BlockSpec(memory_space=pltpu.VMEM)
    hbm = pl.BlockSpec(memory_space=pl.ANY)
    out = jax.ShapeDtypeStruct((1, ROWS, 2 * HALF), F32)
    count = 128
    return pl.pallas_call(
        kernel,
        out_shape=(out, out),
        in_specs=[smem, smem, vmem, vmem, hbm, hbm],
        out_specs=(vmem, vmem),
        scratch_shapes=[
            pltpu.VMEM((2, 4, 4) + block, BF16),
            pltpu.VMEM((2, BROWS, HALF), BF16),
            pltpu.VMEM((2, 4, 4, ROWS, BROWS), F32),
            pltpu.VMEM((4, 4, ROWS, BROWS), BF16),
            pltpu.VMEM((BROWS, BROWS), BF16),
            pltpu.VMEM((2, 4, 4) + block, F32),
            pltpu.VMEM((2, 8) + block, F32),
            pltpu.VMEM((2, 8) + block, F32),
            pltpu.VMEM((2, 8) + block, F32),
            pltpu.VMEM((2, 4, 4) + block, BF16),
            pltpu.VMEM((2, 4) + block, BF16),
            pltpu.VMEM((2, 2, 4) + block, BF16),
            pltpu.VMEM((2, 4) + block, BF16),
            pltpu.VMEM((2,) + block, BF16),
            pltpu.VMEM((2, 2) + block, BF16),
            pltpu.VMEM((2, 8) + block, BF16),
            pltpu.VMEM((2, 8) + block, BF16),
            pltpu.VMEM((2, 2) + block, BF16),
            pltpu.VMEM((4, ROWS, 128), F32),
            pltpu.SemaphoreType.DMA((4,)),
            pltpu.SemaphoreType.DMA((count,)),
            pltpu.SemaphoreType.DMA((count,)),
        ],
        compiler_params=pltpu.CompilerParams(
            collective_id=0, has_side_effects=True, vmem_limit_bytes=66 * 1000 * 1000
        ),
    )(occ_alpha, occ_beta, virt_alpha.reshape(12, 128), virt_beta.reshape(12, 128), orbital_alpha, orbital_beta)


def solution(mesh):
    in_specs = (P("grp", "slab", None), P("grp", "slab", None), P(), P(), P(), P())
    out_specs = (P("grp", "slab", None), P("grp", "slab", None))
    return jax.shard_map(body, mesh=mesh, in_specs=in_specs, out_specs=out_specs, check_vma=False)
```

```python
import functools

import jax
import jax.numpy as jnp
from jax import lax
from jax.experimental import pallas as pl
from jax.experimental.pallas import tpu as pltpu
from jax.sharding import PartitionSpec as P

MESH = pl.DeviceIdType.MESH
ROWS = 48
HALF = 1280
QUART = 640
BROWS = 768
POS = {0: 0, 1: 1, 7: 2, 2: 3, 6: 4, 3: 5, 5: 6, 4: 7}
SCALE = 2.0**41
TINY = 1e-37
F32 = jnp.float32
BF16 = jnp.bfloat16


def kernel(
    occ_a, occ_b, virt_a, virt_b, a_hbm, b_hbm, ga_out, gb_out,
    A, B, I, T, TT, G, GBO, GBS, GBR, S1, R1A, R1B, S2, R2A, R2B, SZ, RZ, RZ0, VA,
    OUT, out_sem, local_sem, send_sem, recv_sem,
):
    grp = lax.axis_index("grp")
    slab = lax.axis_index("slab")
    z_hi, y = grp // 4, grp % 4
    x, z_lo, core = slab // 8, (slab // 2) % 4, slab % 2
    z = z_hi * 4 + z_lo

    def device(dx=0, dy=0, dz=0, dc=0):
        nx, ny, nz, nc = (x + dx) % 4, (y + dy) % 4, (z + dz) % 8, (core + dc) % 2
        return ((nz // 4) * 4 + ny, nx * 8 + (nz % 4) * 2 + nc)

    xy = {(0, 1): device(dx=1), (0, -1): device(dx=3), (1, 1): device(dy=1), (1, -1): device(dy=3)}
    zdev = {1: device(dz=1), -1: device(dz=7)}
    sibling = device(dc=1)

    local = []
    for h in range(2):
        cols = pl.ds(h * HALF, HALF)
        local.append(pltpu.make_async_copy(a_hbm.at[0, :, cols], A.at[h, 0, 0], local_sem.at[h]))
        local.append(pltpu.make_async_copy(b_hbm.at[0, :, cols], B.at[h, pl.ds(0, ROWS)], local_sem.at[2 + h]))
    for copy in local:
        copy.start()

    barrier = pltpu.get_barrier_semaphore()
    for neighbour in list(xy.values()) + list(zdev.values()) + [sibling]:
        pl.semaphore_signal(barrier, inc=1, device_id=neighbour, device_id_type=MESH)

    eye = lax.broadcasted_iota(jnp.int32, (ROWS, 128), 0) == lax.broadcasted_iota(jnp.int32, (ROWS, 128), 1)

    def energies(ref, column):
        return jnp.concatenate([ref[pl.ds(3 * column + i, 1), :] for i in range(3)], axis=1)

    for dx in range(4):
        row = jnp.broadcast_to(energies(virt_a, (x + dx) % 4), (8, 384))
        row = pltpu.roll(row, (384 - 96 * z_lo - 48 * core) % 384, 1)[0:1, :128]
        column = jnp.sum(jnp.where(eye, jnp.broadcast_to(row, (ROWS, 128)), 0.0), axis=1, keepdims=True)
        VA[dx] = jnp.broadcast_to(column, (ROWS, 128))
    lanes = lax.broadcasted_iota(jnp.int32, (8, BROWS), 1)
    part = energies(virt_b, x)
    ring_virt = jnp.broadcast_to(jnp.concatenate([part, part], axis=1), (8, BROWS))
    ring_occ = jnp.where(lanes < 384, occ_b[y], occ_b[4 + y])
    vb = jnp.zeros((8, BROWS), F32)
    ob = jnp.zeros((8, BROWS), F32)
    for r, p in POS.items():
        there = (z + r) % 8
        for k in range(2):
            shift = (96 * p + 768 - 96 * there + (48 * core if k else 768 - 48 * core)) % 768
            here = (lanes >= 96 * p + 48 * k) & (lanes < 96 * p + 48 * k + 48)
            vb = jnp.where(here, pltpu.roll(ring_virt, shift, 1), vb)
            ob = jnp.where(here, pltpu.roll(ring_occ, shift, 1), ob)
    vb, ob = vb[0:1], ob[0:1]

    copies = {}

    def remote(name, src, dst, dev):
        index = len(copies)
        copies[name] = pltpu.make_async_remote_copy(
            src_ref=src, dst_ref=dst, send_sem=send_sem.at[index], recv_sem=recv_sem.at[index],
            device_id=dev, device_id_type=MESH,
        )

    def start(*names):
        for name in names:
            copies[name].start()

    def arrived(*names):
        for name in names:
            copies[name].wait_recv()

    def ablock(h, d1, d2):
        return A.at[0, d2, d1] if h == 0 else A.at[1, d1, d2]

    def bblock(h, r, k=0):
        return B.at[h, pl.ds(POS[r % 8] * 96 + k * ROWS, ROWS)]

    first, second = pl.ds(0, QUART), pl.ds(QUART, QUART)
    for h in range(2):
        one, two = h, 1 - h
        remote(("p1+", h), ablock(h, 0, 0), ablock(h, 3, 0), xy[one, 1])
        remote(("p1-", h), ablock(h, 0, 0), ablock(h, 1, 0), xy[one, -1])
        remote(("p1f+", h), ablock(h, 3, 0).at[:, first], ablock(h, 2, 0).at[:, first], xy[one, 1])
        remote(("p1f-", h), ablock(h, 1, 0).at[:, second], ablock(h, 2, 0).at[:, second], xy[one, -1])
        for u in range(4):
            remote(("p2+", h, u), ablock(h, u, 0), ablock(h, u, 3), xy[two, 1])
            remote(("p2-", h, u), ablock(h, u, 0), ablock(h, u, 1), xy[two, -1])
            if u % 2 == 0:
                remote(("p2f", h, u), ablock(h, u, 3), ablock(h, u, 2), xy[two, 1])
            else:
                remote(("p2f", h, u), ablock(h, u, 1), ablock(h, u, 2), xy[two, -1])
        for k in range(1, 4):
            remote(("z+", h, k), bblock(h, 1 - k), bblock(h, -k), zdev[1])
            remote(("z-", h, k), bblock(h, k - 1), bblock(h, k), zdev[-1])
        if h == 0:
            remote(("z4", h), bblock(h, 5), bblock(h, 4), zdev[1])
        else:
            remote(("z4", h), bblock(h, 3), bblock(h, 4), zdev[-1])
        for r in range(8):
            remote(("sib", h, r), bblock(h, r, 0), bblock(h, r, 1), sibling)

        for u in range(4):
            remote(("1a", h, u), S1.at[h, 2, u], R1A.at[h, u], xy[two, 1 if u % 2 == 0 else -1])
            remote(("1b+", h, u), S1.at[h, 1, u], R1B.at[h, 0, u], xy[two, 1])
            remote(("1b-", h, u), S1.at[h, 3, u], R1B.at[h, 1, u], xy[two, -1])
        remote(("2a+", h), S2.at[h, 2, :, first], R2A.at[h, :, first], xy[one, 1])
        remote(("2a-", h), S2.at[h, 2, :, second], R2A.at[h, :, second], xy[one, -1])
        remote(("2b+", h), S2.at[h, 1], R2B.at[h, 0], xy[one, 1])
        remote(("2b-", h), S2.at[h, 3], R2B.at[h, 1], xy[one, -1])
        if h == 0:
            remote(("rz", h, 4), SZ.at[h, 4], RZ.at[h, 3], zdev[1])
        else:
            remote(("rz", h, 4), SZ.at[h, 4], RZ.at[h, 5], zdev[-1])
        for r in (3, 2):
            remote(("rz", h, r), SZ.at[h, r], RZ.at[h, r - 1], zdev[1])
            remote(("rz", h, 8 - r), SZ.at[h, 8 - r], RZ.at[h, 9 - r], zdev[-1])
        remote(("rz", h, 1), SZ.at[h, 1], RZ0.at[h, 0], zdev[1])
        remote(("rz", h, 7), SZ.at[h, 7], RZ0.at[h, 1], zdev[-1])
        for p in range(8):
            remote(("gsib", h, p), GBS.at[h, p], GBR.at[h, p], sibling)

    def encode(value):
        scaled = value * SCALE
        return (scaled * jnp.abs(scaled)).astype(BF16)

    def decode(code):
        wide = code.astype(F32)
        return wide * lax.rsqrt(jnp.maximum(jnp.abs(wide), TINY)) * (1.0 / SCALE)

    def integrals(h, d2, low, width):
        left = (A[0, d2] if h == 0 else A[1, :, d2]).reshape(4 * ROWS, HALF)
        right = B[h, pl.ds(low, width), :]
        value = lax.dot_general(left, right, (((1,), (1,)), ((), ())), preferred_element_type=F32)
        value = value.reshape(4, ROWS, width)
        if h == 0:
            I[0, d2, :, :, pl.ds(low, width)] = value
        else:
            I[1, :, d2, :, pl.ds(low, width)] = value

    def ratio(number, dy, dx, tile):
        lanes = slice(tile * 128, tile * 128 + 128)
        below = VA[dx] + vb[:, lanes] - occ_a[z_hi * 4 + (y + dy) % 4] - ob[:, lanes]
        return (-number / below).astype(BF16)

    def transpose(tile):
        square = T[:, :, :, pl.ds(tile * 128, 128)].reshape(BROWS, 128)
        TT[pl.ds(tile * 128, 128), :] = jnp.transpose(square.astype(F32)).astype(BF16)

    def amplitudes(low, high):
        def one(block, carry):
            dy, dx = block // 4, block % 4
            for tile in range(low, high):
                at = pl.ds(tile * 128, 128)
                T[dy, dx, :, at] = ratio(I[0, dy, dx, :, at] + I[1, dy, dx, :, at], dy, dx, tile)
            return carry

        lax.fori_loop(0, 16, one, 0)
        for tile in range(low, high):
            transpose(tile)

    def last_amplitudes(dy):
        at = pl.ds(640, 128)
        value = None
        for h in range(2):
            left = A[h, dy].reshape(4 * ROWS, HALF)
            term = lax.dot_general(left, B[h, at, :], (((1,), (1,)), ((), ())), preferred_element_type=F32)
            value = term if value is None else value + term
        for dx in range(4):
            T[dy, dx, :, at] = ratio(value[dx * ROWS:(dx + 1) * ROWS], dy, dx, 5)

    def alpha_term(h, d2):
        raw = {2: (0, 1, 2, 3), 1: (1, 3), 3: (0, 2), 0: ()}[d2]

        def one(j, carry):
            at = pl.ds(pl.multiple_of(j * 256, 256), 256)
            left = (T[d2] if h == 0 else T[:, d2]).reshape(4 * ROWS, BROWS)
            value = jnp.dot(left, B[h, :, at], preferred_element_type=F32)
            for u in range(4):
                block = value[u * ROWS:(u + 1) * ROWS]
                if u in raw:
                    S1[h, d2, u, :, at] = encode(block)
                else:
                    G[h, d2, u, :, at] = block
            return carry

        lax.fori_loop(0, 5, one, 0, unroll=True)

    def beta_term(h, low, high):
        def one(j, carry):
            at = pl.ds(pl.multiple_of(j * 256, 256), 256)
            right = A[h, :, :, :, at].reshape(BROWS, 256)
            value = jnp.dot(TT[pl.ds(low * 96, (high - low) * 96), :], right, preferred_element_type=F32)
            for p in range(low, high):
                base = (p - low) * 96
                GBO[h, p, :, at] = value[base:base + ROWS]
                GBS[h, p, :, at] = value[base + ROWS:base + 2 * ROWS]
            return carry

        lax.fori_loop(0, 5, one, 0, unroll=True)
        for p in range(low, high):
            start(("gsib", h, p))

    def by_rows(body):
        def one(step, carry):
            body(pl.ds(pl.multiple_of(step * 16, 16), 16))
            return carry

        lax.fori_loop(0, ROWS // 16, one, 0)

    for copy in local:
        copy.wait()
    pl.semaphore_wait(barrier, 7)
    H = (0, 1)
    for h in H:
        start(("p1+", h), ("p1-", h))
    for h in H:
        start(("z+", h, 1), ("z-", h, 1))
    for h in H:
        start(("p2+", h, 0), ("p2-", h, 0))
    for h in H:
        start(("sib", h, 0))
    for h in H:
        arrived(("p1+", h), ("p1-", h))
        start(("p1f+", h), ("p1f-", h))
    for u in (3, 1):
        for h in H:
            start(("p2+", h, u), ("p2-", h, u))
    for h in H:
        arrived(("z+", h, 1), ("z-", h, 1))
        start(("z+", h, 2), ("z-", h, 2), ("sib", h, 1), ("sib", h, 7))
    for h in H:
        arrived(("p1f+", h), ("p1f-", h))
        start(("p2+", h, 2), ("p2-", h, 2))
    for h in H:
        arrived(("p2+", h, 0), ("p2-", h, 0))
        start(("p2f", h, 0))
    for h in H:
        arrived(("sib", h, 0), ("sib", h, 1), ("sib", h, 7))
        integrals(h, 0, 0, 256)
    for h in H:
        arrived(("z+", h, 2), ("z-", h, 2))
        start(("z+", h, 3), ("z-", h, 3), ("sib", h, 2), ("sib", h, 6))
    for u in (3, 1):
        for h in H:
            arrived(("p2+", h, u), ("p2-", h, u))
            start(("p2f", h, u))
    for h in H:
        arrived(("p2+", h, 2), ("p2-", h, 2))
        start(("p2f", h, 2))
    for h in H:
        integrals(h, 1, 0, 256)
        integrals(h, 3, 0, 256)
    for h in H:
        arrived(("z+", h, 3), ("z-", h, 3))
        start(("z4", h), ("sib", h, 3), ("sib", h, 5))
    for h in H:
        arrived(("sib", h, 2), ("sib", h, 6), ("sib", h, 3))
        for d2 in (0, 1, 3):
            integrals(h, d2, 256, 256)
    for h in H:
        arrived(("sib", h, 5))
        for d2 in (0, 1, 3):
            integrals(h, d2, 512, 128)
    for h in H:
        arrived(("z4", h))
        start(("sib", h, 4))
    for h in H:
        for u in (0, 3, 1, 2):
            arrived(("p2f", h, u))
        integrals(h, 2, 0, 256)
        integrals(h, 2, 256, 256)
        integrals(h, 2, 512, 128)
    amplitudes(0, 5)
    for h in H:
        arrived(("sib", h, 4))
    for dy in (2, 1, 3, 0):
        last_amplitudes(dy)
    transpose(5)

    outward = {}

    def put(which, h):
        target = (ga_out, gb_out)[which].at[0, :, pl.ds(h * HALF, HALF)]
        outward[which, h] = pltpu.make_async_copy(OUT.at[which, h], target, out_sem.at[which, h])
        outward[which, h].start()

    def add_first(h, u):
        d2 = 1 if u % 2 == 0 else 3
        arrived(("1a", h, u))

        def body(rows):
            S1[h, d2, u, rows] = encode(G[h, d2, u, rows] + decode(R1A[h, u, rows]))

        by_rows(body)
        start(("1b+" if d2 == 1 else "1b-", h, u))

    def plane_sum(h, u, rows):
        return G[h, 0, u, rows] + decode(R1B[h, 0, u, rows]) + decode(R1B[h, 1, u, rows])

    def z_send(h, r):
        p = POS[r]
        chained = r in (1, 2, 6, 7) or (r, h) in ((3, 0), (5, 1))
        arrived(("gsib", h, p))
        if r == 3 and h == 0 or r == 5 and h == 1:
            arrived(("rz", h, 4))
        elif chained:
            arrived(("rz", h, r + 1 if r < 4 else r - 1))

        def body(rows):
            value = GBO[h, p, rows] + GBR[h, p, rows]
            if chained:
                value = value + decode(RZ[h, r, rows])
            SZ[h, r, rows] = encode(value)

        by_rows(body)
        start(("rz", h, r))

    def second_far(h):
        arrived(("1b+", h, 2), ("1b-", h, 2))

        def body(rows):
            S2[h, 2, rows] = encode(plane_sum(h, 2, rows))

        by_rows(body)
        start(("2a+", h), ("2a-", h))

    def second_near(h, u):
        arrived(("1b+", h, u), ("1b-", h, u))
        arrived(("2a+" if u == 1 else "2a-", h))
        added, plain = (first, second) if u == 1 else (second, first)

        def body(rows):
            value = plane_sum(h, u, rows)
            S2[h, u, rows, plain] = encode(value[:, :QUART] if u == 3 else value[:, QUART:])
            value = value[:, QUART:] if u == 3 else value[:, :QUART]
            S2[h, u, rows, added] = encode(value + decode(R2A[h, rows, added]))

        by_rows(body)
        start(("2b+" if u == 1 else "2b-", h))

    for h in H:
        beta_term(h, 7, 8)
    for h in H:
        alpha_term(h, 2)
        for u in (2, 1, 3, 0):
            start(("1a", h, u))
    for h in H:
        z_send(h, 4)
    for h in H:
        alpha_term(h, 1)
        start(("1b+", h, 1), ("1b+", h, 3))
    for h in H:
        alpha_term(h, 3)
        start(("1b-", h, 2), ("1b-", h, 0))
    for h in (1, 0):
        beta_term(h, 5, 7)
    z_send(1, 3)
    z_send(0, 5)
    for h in H:
        add_first(h, 2)
    z_send(0, 3)
    z_send(1, 5)
    for u in (1, 3, 0):
        for h in H:
            add_first(h, u)
    for h in (1, 0):
        beta_term(h, 3, 5)
    for h in H:
        alpha_term(h, 0)
    z_send(1, 2)
    z_send(0, 6)
    z_send(0, 2)
    z_send(1, 6)
    for h in H:
        beta_term(h, 1, 3)
    for h in H:
        beta_term(h, 0, 1)
    for h in H:
        second_far(h)
    z_send(1, 1)
    z_send(0, 7)
    z_send(0, 1)
    z_send(1, 7)
    for h in H:
        second_near(h, 1)
        second_near(h, 3)
    for h in H:
        arrived(("1b+", h, 0), ("1b-", h, 0))

        def body(rows):
            G[h, 0, 0, rows] = plane_sum(h, 0, rows)

        by_rows(body)
    for h in H:
        arrived(("gsib", h, 0), ("rz", h, 1), ("rz", h, 7))

        def body(rows):
            OUT[1, h, rows] = (
                GBO[h, 0, rows] + GBR[h, 0, rows] + decode(RZ0[h, 0, rows]) + decode(RZ0[h, 1, rows])
            )

        by_rows(body)
        put(1, h)
    for h in H:
        arrived(("2b+", h), ("2b-", h))

        def body(rows):
            OUT[0, h, rows] = (
                G[h, 0, 0, rows] + decode(R2B[h, 0, rows]) + decode(R2B[h, 1, rows])
            )

        by_rows(body)
        put(0, h)
    for copy in list(outward.values()):
        copy.wait()
    for copy in copies.values():
        copy.wait_send()


def hand_over(ga_in, gb_in, ga_out, gb_out, held, in_sem, out_sem):
    pairs = [(w, h) for h in range(2) for w in range(2)]
    source, target = (ga_in, gb_in), (ga_out, gb_out)
    inward = [
        pltpu.make_async_copy(source[w].at[0, :, pl.ds(h * HALF, HALF)], held.at[w, h], in_sem.at[w, h])
        for w, h in pairs
    ]
    outward = [
        pltpu.make_async_copy(held.at[w, h], target[w].at[0, :, pl.ds(h * HALF, HALF)], out_sem.at[w, h])
        for w, h in pairs
    ]
    for copy in inward:
        copy.start()
    for before, after in zip(inward, outward):
        before.wait()
        after.start()
    for copy in outward:
        copy.wait()


def body(orbital_alpha, orbital_beta, occ_alpha, occ_beta, virt_alpha, virt_beta):
    block = (ROWS, HALF)
    smem = pl.BlockSpec(memory_space=pltpu.SMEM)
    vmem = pl.BlockSpec(memory_space=pltpu.VMEM)
    hbm = pl.BlockSpec(memory_space=pl.ANY)
    out = jax.ShapeDtypeStruct((1, ROWS, 2 * HALF), F32)
    count = 128
    sums = pl.pallas_call(
        kernel,
        out_shape=(out, out),
        in_specs=[smem, smem, vmem, vmem, hbm, hbm],
        out_specs=(hbm, hbm),
        scratch_shapes=[
            pltpu.VMEM((2, 4, 4) + block, BF16),
            pltpu.VMEM((2, BROWS, HALF), BF16),
            pltpu.VMEM((2, 4, 4, ROWS, BROWS), F32),
            pltpu.VMEM((4, 4, ROWS, BROWS), BF16),
            pltpu.VMEM((BROWS, BROWS), BF16),
            pltpu.VMEM((2, 4, 4) + block, F32),
            pltpu.VMEM((2, 8) + block, F32),
            pltpu.VMEM((2, 8) + block, F32),
            pltpu.VMEM((2, 8) + block, F32),
            pltpu.VMEM((2, 4, 4) + block, BF16),
            pltpu.VMEM((2, 4) + block, BF16),
            pltpu.VMEM((2, 2, 4) + block, BF16),
            pltpu.VMEM((2, 4) + block, BF16),
            pltpu.VMEM((2,) + block, BF16),
            pltpu.VMEM((2, 2) + block, BF16),
            pltpu.VMEM((2, 8) + block, BF16),
            pltpu.VMEM((2, 8) + block, BF16),
            pltpu.VMEM((2, 2) + block, BF16),
            pltpu.VMEM((4, ROWS, 128), F32),
            pltpu.VMEM((2, 2) + block, F32),
            pltpu.SemaphoreType.DMA((2, 2)),
            pltpu.SemaphoreType.DMA((4,)),
            pltpu.SemaphoreType.DMA((count,)),
            pltpu.SemaphoreType.DMA((count,)),
        ],
        compiler_params=pltpu.CompilerParams(
            collective_id=0, has_side_effects=True, vmem_limit_bytes=66 * 1000 * 1000
        ),
    )(occ_alpha, occ_beta, virt_alpha.reshape(12, 128), virt_beta.reshape(12, 128), orbital_alpha, orbital_beta)
    return pl.pallas_call(
        hand_over,
        out_shape=(out, out),
        in_specs=[hbm, hbm],
        out_specs=(hbm, hbm),
        scratch_shapes=[
            pltpu.VMEM((2, 2) + block, F32),
            pltpu.SemaphoreType.DMA((2, 2)),
            pltpu.SemaphoreType.DMA((2, 2)),
        ],
        compiler_params=pltpu.CompilerParams(vmem_limit_bytes=66 * 1000 * 1000),
    )(*sums)


def solution(mesh):
    in_specs = (P("grp", "slab", None), P("grp", "slab", None), P(), P(), P(), P())
    out_specs = (P("grp", "slab", None), P("grp", "slab", None))
    return jax.shard_map(body, mesh=mesh, in_specs=in_specs, out_specs=out_specs, check_vma=False)
```

```python
import functools

import jax
import jax.numpy as jnp
from jax import lax
from jax.experimental import pallas as pl
from jax.experimental.pallas import tpu as pltpu
from jax.sharding import PartitionSpec as P

MESH = pl.DeviceIdType.MESH
ROWS = 48
HALF = 1280
QUART = 640
BROWS = 768
POS = {0: 0, 1: 1, 7: 2, 2: 3, 6: 4, 3: 5, 5: 6, 4: 7}
SCALE = 2.0**41
TINY = 1e-37
F32 = jnp.float32
BF16 = jnp.bfloat16


def kernel(
    occ_a, occ_b, virt_a, virt_b, a_hbm, b_hbm, ga_out, gb_out,
    A, B, I, T, TT, G, GBO, GBS, GBR, S1, R1A, R1B, S2, R2A, R2B, SZ, RZ, RZ0, VA, RD,
    OUT, out_sem, local_sem, send_sem, recv_sem,
):
    grp = lax.axis_index("grp")
    slab = lax.axis_index("slab")
    z_hi, y = grp // 4, grp % 4
    x, z_lo, core = slab // 8, (slab // 2) % 4, slab % 2
    z = z_hi * 4 + z_lo

    def device(dx=0, dy=0, dz=0, dc=0):
        nx, ny, nz, nc = (x + dx) % 4, (y + dy) % 4, (z + dz) % 8, (core + dc) % 2
        return ((nz // 4) * 4 + ny, nx * 8 + (nz % 4) * 2 + nc)

    xy = {(0, 1): device(dx=1), (0, -1): device(dx=3), (1, 1): device(dy=1), (1, -1): device(dy=3)}
    zdev = {1: device(dz=1), -1: device(dz=7)}
    sibling = device(dc=1)

    local = []
    for h in range(2):
        cols = pl.ds(h * HALF, HALF)
        local.append(pltpu.make_async_copy(a_hbm.at[0, :, cols], A.at[h, 0, 0], local_sem.at[h]))
        local.append(pltpu.make_async_copy(b_hbm.at[0, :, cols], B.at[h, pl.ds(0, ROWS)], local_sem.at[2 + h]))
    for copy in local:
        copy.start()

    barrier = pltpu.get_barrier_semaphore()
    for neighbour in list(xy.values()) + list(zdev.values()) + [sibling]:
        pl.semaphore_signal(barrier, inc=1, device_id=neighbour, device_id_type=MESH)

    copies = {}

    def remote(name, src, dst, dev):
        index = len(copies)
        copies[name] = pltpu.make_async_remote_copy(
            src_ref=src, dst_ref=dst, send_sem=send_sem.at[index], recv_sem=recv_sem.at[index],
            device_id=dev, device_id_type=MESH,
        )

    def start(*names):
        for name in names:
            copies[name].start()

    def arrived(*names):
        for name in names:
            copies[name].wait_recv()

    def ablock(h, d1, d2):
        return A.at[0, d2, d1] if h == 0 else A.at[1, d1, d2]

    def bblock(h, r, k=0):
        return B.at[h, pl.ds(POS[r % 8] * 96 + k * ROWS, ROWS)]

    first, second = pl.ds(0, QUART), pl.ds(QUART, QUART)
    for h in range(2):
        one, two = h, 1 - h
        remote(("p1+", h), ablock(h, 0, 0), ablock(h, 3, 0), xy[one, 1])
        remote(("p1-", h), ablock(h, 0, 0), ablock(h, 1, 0), xy[one, -1])
        remote(("p1f+", h), ablock(h, 3, 0).at[:, first], ablock(h, 2, 0).at[:, first], xy[one, 1])
        remote(("p1f-", h), ablock(h, 1, 0).at[:, second], ablock(h, 2, 0).at[:, second], xy[one, -1])
        for u in range(4):
            remote(("p2+", h, u), ablock(h, u, 0), ablock(h, u, 3), xy[two, 1])
            remote(("p2-", h, u), ablock(h, u, 0), ablock(h, u, 1), xy[two, -1])
            if u % 2 == 0:
                remote(("p2f", h, u), ablock(h, u, 3), ablock(h, u, 2), xy[two, 1])
            else:
                remote(("p2f", h, u), ablock(h, u, 1), ablock(h, u, 2), xy[two, -1])
        for r in range(8):
            remote(("sib", h, r), bblock(h, r, 0), bblock(h, r, 1), sibling)

        for u in range(4):
            remote(("1a", h, u), S1.at[h, 2, u], R1A.at[h, u], xy[two, 1 if u % 2 == 0 else -1])
            remote(("1b+", h, u), S1.at[h, 1, u], R1B.at[h, 0, u], xy[two, 1])
            remote(("1b-", h, u), S1.at[h, 3, u], R1B.at[h, 1, u], xy[two, -1])
        remote(("2a+", h), S2.at[h, 2, :, first], R2A.at[h, :, first], xy[one, 1])
        remote(("2a-", h), S2.at[h, 2, :, second], R2A.at[h, :, second], xy[one, -1])
        remote(("2b+", h), S2.at[h, 1], R2B.at[h, 0], xy[one, 1])
        remote(("2b-", h), S2.at[h, 3], R2B.at[h, 1], xy[one, -1])
        for p in range(8):
            remote(("gsib", h, p), GBS.at[h, p], GBR.at[h, p], sibling)

    for q in range(4):
        h, cols = q // 2, (first, second)[q % 2]

        def bquarter(r):
            return bblock(h, r).at[:, cols]

        for k in range(1, 4):
            remote(("z+", q, k), bquarter(1 - k), bquarter(-k), zdev[1])
            remote(("z-", q, k), bquarter(k - 1), bquarter(k), zdev[-1])
        if h == 0:
            remote(("z4", q), bquarter(5), bquarter(4), zdev[1])
            remote(("rz", q, 4), SZ.at[q, 4], RZ.at[q, 3], zdev[1])
        else:
            remote(("z4", q), bquarter(3), bquarter(4), zdev[-1])
            remote(("rz", q, 4), SZ.at[q, 4], RZ.at[q, 5], zdev[-1])
        for r in (3, 2):
            remote(("rz", q, r), SZ.at[q, r], RZ.at[q, r - 1], zdev[1])
            remote(("rz", q, 8 - r), SZ.at[q, 8 - r], RZ.at[q, 9 - r], zdev[-1])
        remote(("rz", q, 1), SZ.at[q, 1], RZ0.at[q, 0], zdev[1])
        remote(("rz", q, 7), SZ.at[q, 7], RZ0.at[q, 1], zdev[-1])

    def encode(value):
        scaled = value * SCALE
        return (scaled * jnp.abs(scaled)).astype(BF16)

    def decode(code):
        wide = code.astype(F32)
        return wide * lax.rsqrt(jnp.maximum(jnp.abs(wide), TINY)) * (1.0 / SCALE)

    def integrals(h, d2, low, width):
        left = (A[0, d2] if h == 0 else A[1, :, d2]).reshape(4 * ROWS, HALF)
        right = B[h, pl.ds(low, width), :]
        value = lax.dot_general(left, right, (((1,), (1,)), ((), ())), preferred_element_type=F32)
        value = value.reshape(4, ROWS, width)
        if h == 0:
            I[0, d2, :, :, pl.ds(low, width)] = value
        else:
            I[1, :, d2, :, pl.ds(low, width)] = value

    def ratio(number, dy, dx, tile):
        return (number * RD[dy, dx, :, pl.ds(tile * 128, 128)]).astype(BF16)

    def transpose(tile):
        square = T[:, :, :, pl.ds(tile * 128, 128)].reshape(BROWS, 128)
        TT[pl.ds(tile * 128, 128), :] = jnp.transpose(square.astype(F32)).astype(BF16)

    def amplitudes(count, place):
        def one(block, carry):
            dy, dx = place(block)
            for tile in range(5):
                at = pl.ds(tile * 128, 128)
                T[dy, dx, :, at] = ratio(I[0, dy, dx, :, at] + I[1, dy, dx, :, at], dy, dx, tile)
            return carry

        lax.fori_loop(0, count, one, 0)

    def near(index):
        return index + index // 2

    def near_place(block):
        return near(block // 3), near(block % 3)

    def far_place(block):
        row = block < 4
        return jnp.where(row, 2, near(block - 4)), jnp.where(row, block, 2)

    def last_amplitudes(dy):
        at = pl.ds(640, 128)
        value = None
        for h in range(2):
            left = A[h, dy].reshape(4 * ROWS, HALF)
            term = lax.dot_general(left, B[h, at, :], (((1,), (1,)), ((), ())), preferred_element_type=F32)
            value = term if value is None else value + term
        for dx in range(4):
            T[dy, dx, :, at] = ratio(value[dx * ROWS:(dx + 1) * ROWS], dy, dx, 5)

    def alpha_term(h, d2):
        raw = {2: (0, 1, 2, 3), 1: (1, 3), 3: (0, 2), 0: ()}[d2]

        def one(j, carry):
            at = pl.ds(pl.multiple_of(j * 256, 256), 256)
            left = (T[d2] if h == 0 else T[:, d2]).reshape(4 * ROWS, BROWS)
            value = jnp.dot(left, B[h, :, at], preferred_element_type=F32)
            for u in range(4):
                block = value[u * ROWS:(u + 1) * ROWS]
                if u in raw:
                    S1[h, d2, u, :, at] = encode(block)
                else:
                    G[h, d2, u, :, at] = block
            return carry

        lax.fori_loop(0, 5, one, 0, unroll=True)

    def beta_term(h, low, high):
        def one(j, carry):
            at = pl.ds(pl.multiple_of(j * 256, 256), 256)
            right = A[h, :, :, :, at].reshape(BROWS, 256)
            value = jnp.dot(TT[pl.ds(low * 96, (high - low) * 96), :], right, preferred_element_type=F32)
            for p in range(low, high):
                base = (p - low) * 96
                GBO[h, p, :, at] = value[base:base + ROWS]
                GBS[h, p, :, at] = value[base + ROWS:base + 2 * ROWS]
            return carry

        lax.fori_loop(0, 5, one, 0, unroll=True)
        for p in range(low, high):
            start(("gsib", h, p))

    def by_rows(body):
        def one(step, carry):
            body(pl.ds(pl.multiple_of(step * 16, 16), 16))
            return carry

        lax.fori_loop(0, ROWS // 16, one, 0)

    for copy in local:
        copy.wait()
    pl.semaphore_wait(barrier, 7)
    H = (0, 1)
    def z_pass(k, q):
        h = q // 2
        arrived(("z+", q, k), ("z-", q, k))
        if k < 3:
            start(("z+", q, k + 1), ("z-", q, k + 1))
        else:
            start(("z4", q))
        if q % 2 == 1:
            start(("sib", h, k), ("sib", h, 8 - k))

    for h in H:
        start(("p1+", h), ("p1-", h))
    for q in range(4):
        start(("z+", q, 1), ("z-", q, 1))
    for h in H:
        start(("p2+", h, 0), ("p2-", h, 0))
    for h in H:
        start(("sib", h, 0))

    eye = lax.broadcasted_iota(jnp.int32, (ROWS, 128), 0) == lax.broadcasted_iota(jnp.int32, (ROWS, 128), 1)

    def energies(ref, column):
        return jnp.concatenate([ref[pl.ds(3 * column + i, 1), :] for i in range(3)], axis=1)

    for dx in range(4):
        row = jnp.broadcast_to(energies(virt_a, (x + dx) % 4), (8, 384))
        row = pltpu.roll(row, (384 - 96 * z_lo - 48 * core) % 384, 1)[0:1, :128]
        column = jnp.sum(jnp.where(eye, jnp.broadcast_to(row, (ROWS, 128)), 0.0), axis=1, keepdims=True)
        VA[dx] = jnp.broadcast_to(column, (ROWS, 128))
    lanes = lax.broadcasted_iota(jnp.int32, (8, BROWS), 1)
    part = energies(virt_b, x)
    ring_virt = jnp.broadcast_to(jnp.concatenate([part, part], axis=1), (8, BROWS))
    ring_occ = jnp.where(lanes < 384, occ_b[y], occ_b[4 + y])
    vb = jnp.zeros((8, BROWS), F32)
    ob = jnp.zeros((8, BROWS), F32)
    for r, p in POS.items():
        there = (z + r) % 8
        for k in range(2):
            shift = (96 * p + 768 - 96 * there + (48 * core if k else 768 - 48 * core)) % 768
            here = (lanes >= 96 * p + 48 * k) & (lanes < 96 * p + 48 * k + 48)
            vb = jnp.where(here, pltpu.roll(ring_virt, shift, 1), vb)
            ob = jnp.where(here, pltpu.roll(ring_occ, shift, 1), ob)
    vb, ob = vb[0:1], ob[0:1]

    def inverses(block, carry):
        dy, dx = block // 4, block % 4
        occ = occ_a[z_hi * 4 + (y + dy) % 4]
        for tile in range(6):
            lanes = slice(tile * 128, tile * 128 + 128)
            RD[dy, dx, :, pl.ds(tile * 128, 128)] = -1.0 / (VA[dx] + vb[:, lanes] - occ - ob[:, lanes])
        return carry

    lax.fori_loop(0, 16, inverses, 0)

    z_pass(1, 0)
    for h in H:
        arrived(("p1+", h), ("p1-", h))
        start(("p1f+", h), ("p1f-", h))
    for u in (3, 1):
        for h in H:
            start(("p2+", h, u), ("p2-", h, u))
    z_pass(1, 1)
    z_pass(1, 2)
    z_pass(1, 3)
    z_pass(2, 0)
    for h in H:
        arrived(("p1f+", h), ("p1f-", h))
        start(("p2+", h, 2), ("p2-", h, 2))
    for h in H:
        arrived(("p2+", h, 0), ("p2-", h, 0))
        start(("p2f", h, 0))
    z_pass(2, 1)
    for h in H:
        arrived(("sib", h, 0), ("sib", h, 1), ("sib", h, 7))
        integrals(h, 0, 0, 256)
    z_pass(2, 2)
    for h in H:
        arrived(("p2+", h, 3), ("p2-", h, 3))
        start(("p2f", h, 3))
    z_pass(2, 3)
    z_pass(3, 0)
    for h in H:
        arrived(("p2+", h, 1), ("p2-", h, 1))
        start(("p2f", h, 1))
    z_pass(3, 1)
    z_pass(3, 2)
    for h in H:
        arrived(("p2+", h, 2), ("p2-", h, 2))
        start(("p2f", h, 2))
    z_pass(3, 3)
    for h in H:
        integrals(h, 1, 0, 256)
        integrals(h, 3, 0, 256)
    for h in H:
        arrived(("sib", h, 2), ("sib", h, 6), ("sib", h, 3))
        for d2 in (0, 1, 3):
            integrals(h, d2, 256, 256)
    for h in H:
        arrived(("z4", 2 * h), ("z4", 2 * h + 1))
        start(("sib", h, 4))
    for h in H:
        arrived(("sib", h, 5))
        for d2 in (0, 1, 3):
            integrals(h, d2, 512, 128)
    amplitudes(9, near_place)
    for h in H:
        for u in (0, 3, 1, 2):
            arrived(("p2f", h, u))
        integrals(h, 2, 0, 256)
        integrals(h, 2, 256, 256)
        integrals(h, 2, 512, 128)
    for h in H:
        arrived(("sib", h, 4))
    for dy in range(4):
        last_amplitudes(dy)
    transpose(5)

    outward = {}

    def put(which, h):
        target = (ga_out, gb_out)[which].at[0, :, pl.ds(h * HALF, HALF)]
        outward[which, h] = pltpu.make_async_copy(OUT.at[which, h], target, out_sem.at[which, h])
        outward[which, h].start()

    def add_first(h, u):
        d2 = 1 if u % 2 == 0 else 3
        arrived(("1a", h, u))

        def body(rows):
            S1[h, d2, u, rows] = encode(G[h, d2, u, rows] + decode(R1A[h, u, rows]))

        by_rows(body)
        start(("1b+" if d2 == 1 else "1b-", h, u))

    def plane_sum(h, u, rows):
        return G[h, 0, u, rows] + decode(R1B[h, 0, u, rows]) + decode(R1B[h, 1, u, rows])

    def z_send(q, r):
        h, p, cols = q // 2, POS[r], (first, second)[q % 2]
        chained = r in (1, 2, 6, 7) or (r, h) in ((3, 0), (5, 1))
        if q % 2 == 0:
            arrived(("gsib", h, p))
        if (r, h) in ((3, 0), (5, 1)):
            arrived(("rz", q, 4))
        elif chained:
            arrived(("rz", q, r + 1 if r < 4 else r - 1))

        def body(rows):
            value = GBO[h, p, rows, cols] + GBR[h, p, rows, cols]
            if chained:
                value = value + decode(RZ[q, r, rows])
            SZ[q, r, rows] = encode(value)

        by_rows(body)
        start(("rz", q, r))

    steps = [((0, 4), (2, 4)), ((1, 4), (3, 4)), ((2, 3), (0, 5)), ((3, 3), (1, 5))]
    for r in (3, 2, 1):
        steps += [((0, r), (2, 8 - r)), ((1, r), (3, 8 - r))]
        if r > 1:
            steps += [((2, r - 1), (0, 9 - r)), ((3, r - 1), (1, 9 - r))]

    def z_step(index):
        for q, r in steps[index]:
            z_send(q, r)

    def second_far(h):
        arrived(("1b+", h, 2), ("1b-", h, 2))

        def body(rows):
            S2[h, 2, rows] = encode(plane_sum(h, 2, rows))

        by_rows(body)
        start(("2a+", h), ("2a-", h))

    def second_near(h, u):
        arrived(("1b+", h, u), ("1b-", h, u))
        arrived(("2a+" if u == 1 else "2a-", h))
        added, plain = (first, second) if u == 1 else (second, first)

        def body(rows):
            value = plane_sum(h, u, rows)
            S2[h, u, rows, plain] = encode(value[:, :QUART] if u == 3 else value[:, QUART:])
            value = value[:, QUART:] if u == 3 else value[:, :QUART]
            S2[h, u, rows, added] = encode(value + decode(R2A[h, rows, added]))

        by_rows(body)
        start(("2b+" if u == 1 else "2b-", h))

    for h in H:
        beta_term(h, 7, 8)
    amplitudes(7, far_place)
    for tile in range(5):
        transpose(tile)
    for h in H:
        alpha_term(h, 2)
        for u in (2, 1, 3, 0):
            start(("1a", h, u))
        if h == 0:
            z_step(0)
    beta_term(1, 5, 7)
    z_step(1)
    beta_term(0, 5, 7)
    for h in H:
        alpha_term(h, 3)
        start(("1b-", h, 2))
    z_step(2)
    alpha_term(0, 1)
    z_step(3)
    alpha_term(1, 1)
    beta_term(1, 3, 5)
    z_step(4)
    for h in H:
        add_first(h, 2)
        start(("1b+", h, 1))
    z_step(5)
    for h in H:
        add_first(h, 1)
    beta_term(0, 3, 5)
    z_step(6)
    for h in H:
        start(("1b+", h, 3))
        add_first(h, 3)
    z_step(7)
    for h in H:
        alpha_term(h, 0)
    beta_term(1, 1, 3)
    z_step(8)
    beta_term(0, 1, 3)
    for h in H:
        second_far(h)
    for h in H:
        start(("1b-", h, 0))
        add_first(h, 0)
    z_step(9)
    z_step(10)
    for h in H:
        beta_term(h, 0, 1)
    z_step(11)
    z_step(12)
    for h in H:
        second_near(h, 1)
        second_near(h, 3)
    z_step(13)
    for h in H:
        arrived(("1b+", h, 0), ("1b-", h, 0))

        def body(rows):
            G[h, 0, 0, rows] = plane_sum(h, 0, rows)

        by_rows(body)
    for h in H:
        arrived(("gsib", h, 0))
        for q in (2 * h, 2 * h + 1):
            arrived(("rz", q, 1), ("rz", q, 7))

        def body(rows):
            for part, cols in enumerate((first, second)):
                q = 2 * h + part
                OUT[1, h, rows, cols] = (
                    GBO[h, 0, rows, cols] + GBR[h, 0, rows, cols] + decode(RZ0[q, 0, rows]) + decode(RZ0[q, 1, rows])
                )

        by_rows(body)
        put(1, h)
    for h in H:
        arrived(("2b+", h), ("2b-", h))

        def body(rows):
            OUT[0, h, rows] = (
                G[h, 0, 0, rows] + decode(R2B[h, 0, rows]) + decode(R2B[h, 1, rows])
            )

        by_rows(body)
        put(0, h)
    for copy in list(outward.values()):
        copy.wait()
    for copy in copies.values():
        copy.wait_send()


def hand_over(ga_in, gb_in, ga_out, gb_out, held, in_sem, out_sem):
    pairs = [(w, h) for h in range(2) for w in range(2)]
    source, target = (ga_in, gb_in), (ga_out, gb_out)
    inward = [
        pltpu.make_async_copy(source[w].at[0, :, pl.ds(h * HALF, HALF)], held.at[w, h], in_sem.at[w, h])
        for w, h in pairs
    ]
    outward = [
        pltpu.make_async_copy(held.at[w, h], target[w].at[0, :, pl.ds(h * HALF, HALF)], out_sem.at[w, h])
        for w, h in pairs
    ]
    for copy in inward:
        copy.start()
    for before, after in zip(inward, outward):
        before.wait()
        after.start()
    for copy in outward:
        copy.wait()


def body(orbital_alpha, orbital_beta, occ_alpha, occ_beta, virt_alpha, virt_beta):
    block = (ROWS, HALF)
    smem = pl.BlockSpec(memory_space=pltpu.SMEM)
    vmem = pl.BlockSpec(memory_space=pltpu.VMEM)
    hbm = pl.BlockSpec(memory_space=pl.ANY)
    out = jax.ShapeDtypeStruct((1, ROWS, 2 * HALF), F32)
    count = 160
    sums = pl.pallas_call(
        kernel,
        out_shape=(out, out),
        in_specs=[smem, smem, vmem, vmem, hbm, hbm],
        out_specs=(hbm, hbm),
        scratch_shapes=[
            pltpu.VMEM((2, 4, 4) + block, BF16),
            pltpu.VMEM((2, BROWS, HALF), BF16),
            pltpu.VMEM((2, 4, 4, ROWS, BROWS), F32),
            pltpu.VMEM((4, 4, ROWS, BROWS), BF16),
            pltpu.VMEM((BROWS, BROWS), BF16),
            pltpu.VMEM((2, 4, 4) + block, F32),
            pltpu.VMEM((2, 8) + block, F32),
            pltpu.VMEM((2, 8) + block, F32),
            pltpu.VMEM((2, 8) + block, F32),
            pltpu.VMEM((2, 4, 4) + block, BF16),
            pltpu.VMEM((2, 4) + block, BF16),
            pltpu.VMEM((2, 2, 4) + block, BF16),
            pltpu.VMEM((2, 4) + block, BF16),
            pltpu.VMEM((2,) + block, BF16),
            pltpu.VMEM((2, 2) + block, BF16),
            pltpu.VMEM((4, 8, ROWS, QUART), BF16),
            pltpu.VMEM((4, 8, ROWS, QUART), BF16),
            pltpu.VMEM((4, 2, ROWS, QUART), BF16),
            pltpu.VMEM((4, ROWS, 128), F32),
            pltpu.VMEM((4, 4, ROWS, BROWS), F32),
            pltpu.VMEM((2, 2) + block, F32),
            pltpu.SemaphoreType.DMA((2, 2)),
            pltpu.SemaphoreType.DMA((4,)),
            pltpu.SemaphoreType.DMA((count,)),
            pltpu.SemaphoreType.DMA((count,)),
        ],
        compiler_params=pltpu.CompilerParams(
            collective_id=0, has_side_effects=True, vmem_limit_bytes=66 * 1000 * 1000
        ),
    )(occ_alpha, occ_beta, virt_alpha.reshape(12, 128), virt_beta.reshape(12, 128), orbital_alpha, orbital_beta)
    return pl.pallas_call(
        hand_over,
        out_shape=(out, out),
        in_specs=[hbm, hbm],
        out_specs=(hbm, hbm),
        scratch_shapes=[
            pltpu.VMEM((2, 2) + block, F32),
            pltpu.SemaphoreType.DMA((2, 2)),
            pltpu.SemaphoreType.DMA((2, 2)),
        ],
        compiler_params=pltpu.CompilerParams(vmem_limit_bytes=66 * 1000 * 1000),
    )(*sums)


def solution(mesh):
    in_specs = (P("grp", "slab", None), P("grp", "slab", None), P(), P(), P(), P())
    out_specs = (P("grp", "slab", None), P("grp", "slab", None))
    return jax.shard_map(body, mesh=mesh, in_specs=in_specs, out_specs=out_specs, check_vma=False)
```

```python
import functools

import jax
import jax.numpy as jnp
from jax import lax
from jax.experimental import pallas as pl
from jax.experimental.pallas import tpu as pltpu
from jax.sharding import PartitionSpec as P

MESH = pl.DeviceIdType.MESH
ROWS = 48
HALF = 1280
QUART = 640
BROWS = 768
POS = {0: 0, 1: 1, 7: 2, 2: 3, 6: 4, 3: 5, 5: 6, 4: 7}
SCALE = 2.0**41
TINY = 1e-37
F32 = jnp.float32
BF16 = jnp.bfloat16


def kernel(
    occ_a, occ_b, virt_a, virt_b, a_hbm, b_hbm, ga_out, gb_out,
    A, B, I, T, TT, G, GBO, GBS, GBR, S1, R1A, R1B, S2, R2A, R2B, SZ, RZ, RZ0, VA, RD,
    OUT, out_sem, local_sem, send_sem, recv_sem,
):
    grp = lax.axis_index("grp")
    slab = lax.axis_index("slab")
    z_hi, y = grp // 4, grp % 4
    x, z_lo, core = slab // 8, (slab // 2) % 4, slab % 2
    z = z_hi * 4 + z_lo

    def device(dx=0, dy=0, dz=0, dc=0):
        nx, ny, nz, nc = (x + dx) % 4, (y + dy) % 4, (z + dz) % 8, (core + dc) % 2
        return ((nz // 4) * 4 + ny, nx * 8 + (nz % 4) * 2 + nc)

    xy = {(0, 1): device(dx=1), (0, -1): device(dx=3), (1, 1): device(dy=1), (1, -1): device(dy=3)}
    zdev = {1: device(dz=1), -1: device(dz=7)}
    sibling = device(dc=1)

    local = []
    for h in range(2):
        cols = pl.ds(h * HALF, HALF)
        local.append(pltpu.make_async_copy(a_hbm.at[0, :, cols], A.at[h, 0, 0], local_sem.at[h]))
        local.append(pltpu.make_async_copy(b_hbm.at[0, :, cols], B.at[h, pl.ds(0, ROWS)], local_sem.at[2 + h]))
    for copy in local:
        copy.start()

    barrier = pltpu.get_barrier_semaphore()
    for neighbour in list(xy.values()) + list(zdev.values()) + [sibling]:
        pl.semaphore_signal(barrier, inc=1, device_id=neighbour, device_id_type=MESH)

    copies = {}

    def remote(name, src, dst, dev):
        index = len(copies)
        copies[name] = pltpu.make_async_remote_copy(
            src_ref=src, dst_ref=dst, send_sem=send_sem.at[index], recv_sem=recv_sem.at[index],
            device_id=dev, device_id_type=MESH,
        )

    def start(*names):
        for name in names:
            copies[name].start()

    def arrived(*names):
        for name in names:
            copies[name].wait_recv()

    def ablock(h, d1, d2):
        return A.at[0, d2, d1] if h == 0 else A.at[1, d1, d2]

    def bblock(h, r, k=0):
        return B.at[h, pl.ds(POS[r % 8] * 96 + k * ROWS, ROWS)]

    first, second = pl.ds(0, QUART), pl.ds(QUART, QUART)
    for h in range(2):
        one, two = h, 1 - h
        remote(("p1+", h), ablock(h, 0, 0), ablock(h, 3, 0), xy[one, 1])
        remote(("p1-", h), ablock(h, 0, 0), ablock(h, 1, 0), xy[one, -1])
        remote(("p1f+", h), ablock(h, 3, 0).at[:, first], ablock(h, 2, 0).at[:, first], xy[one, 1])
        remote(("p1f-", h), ablock(h, 1, 0).at[:, second], ablock(h, 2, 0).at[:, second], xy[one, -1])
        for u in range(4):
            remote(("p2+", h, u), ablock(h, u, 0), ablock(h, u, 3), xy[two, 1])
            remote(("p2-", h, u), ablock(h, u, 0), ablock(h, u, 1), xy[two, -1])
            if u % 2 == 0:
                remote(("p2f", h, u), ablock(h, u, 3), ablock(h, u, 2), xy[two, 1])
            else:
                remote(("p2f", h, u), ablock(h, u, 1), ablock(h, u, 2), xy[two, -1])
        for r in range(8):
            remote(("sib", h, r), bblock(h, r, 0), bblock(h, r, 1), sibling)

        for u in range(4):
            remote(("1a", h, u), S1.at[h, 2, u], R1A.at[h, u], xy[two, 1 if u % 2 == 0 else -1])
            remote(("1b+", h, u), S1.at[h, 1, u], R1B.at[h, 0, u], xy[two, 1])
            remote(("1b-", h, u), S1.at[h, 3, u], R1B.at[h, 1, u], xy[two, -1])
        remote(("2a+", h), S2.at[h, 2, :, first], R2A.at[h, :, first], xy[one, 1])
        remote(("2a-", h), S2.at[h, 2, :, second], R2A.at[h, :, second], xy[one, -1])
        remote(("2b+", h), S2.at[h, 1], R2B.at[h, 0], xy[one, 1])
        remote(("2b-", h), S2.at[h, 3], R2B.at[h, 1], xy[one, -1])
        for p in range(8):
            remote(("gsib", h, p), GBS.at[h, p], GBR.at[h, p], sibling)

    for q in range(4):
        h, cols = q // 2, (first, second)[q % 2]

        def bquarter(r):
            return bblock(h, r).at[:, cols]

        for k in range(1, 4):
            remote(("z+", q, k), bquarter(1 - k), bquarter(-k), zdev[1])
            remote(("z-", q, k), bquarter(k - 1), bquarter(k), zdev[-1])
        if h == 0:
            remote(("z4", q), bquarter(5), bquarter(4), zdev[1])
            remote(("rz", q, 4), SZ.at[q, 4], RZ.at[q, 3], zdev[1])
        else:
            remote(("z4", q), bquarter(3), bquarter(4), zdev[-1])
            remote(("rz", q, 4), SZ.at[q, 4], RZ.at[q, 5], zdev[-1])
        for r in (3, 2):
            remote(("rz", q, r), SZ.at[q, r], RZ.at[q, r - 1], zdev[1])
            remote(("rz", q, 8 - r), SZ.at[q, 8 - r], RZ.at[q, 9 - r], zdev[-1])
        remote(("rz", q, 1), SZ.at[q, 1], RZ0.at[q, 0], zdev[1])
        remote(("rz", q, 7), SZ.at[q, 7], RZ0.at[q, 1], zdev[-1])

    def encode(value):
        scaled = value * SCALE
        return (scaled * jnp.abs(scaled)).astype(BF16)

    def decode(code):
        wide = code.astype(F32)
        return wide * lax.rsqrt(jnp.maximum(jnp.abs(wide), TINY)) * (1.0 / SCALE)

    def integrals(h, d2, low, width):
        left = (A[0, d2] if h == 0 else A[1, :, d2]).reshape(4 * ROWS, HALF)
        right = B[h, pl.ds(low, width), :]
        value = lax.dot_general(left, right, (((1,), (1,)), ((), ())), preferred_element_type=F32)
        value = value.reshape(4, ROWS, width)
        if h == 0:
            I[0, d2, :, :, pl.ds(low, width)] = value
        else:
            I[1, :, d2, :, pl.ds(low, width)] = value

    def ratio(number, dy, dx, tile):
        return (number * RD[dy, dx, :, pl.ds(tile * 128, 128)]).astype(BF16)

    def transpose(tile):
        square = T[:, :, :, pl.ds(tile * 128, 128)].reshape(BROWS, 128)
        TT[pl.ds(tile * 128, 128), :] = jnp.transpose(square.astype(F32)).astype(BF16)

    def amplitudes(count, place):
        def one(block, carry):
            dy, dx = place(block)
            for tile in range(5):
                at = pl.ds(tile * 128, 128)
                T[dy, dx, :, at] = ratio(I[0, dy, dx, :, at] + I[1, dy, dx, :, at], dy, dx, tile)
            return carry

        lax.fori_loop(0, count, one, 0)

    def near(index):
        return index + index // 2

    def near_place(block):
        return near(block // 3), near(block % 3)

    def far_place(block):
        row = block < 4
        return jnp.where(row, 2, near(block - 4)), jnp.where(row, block, 2)

    def last_amplitudes(dy):
        at = pl.ds(640, 128)
        value = None
        for h in range(2):
            left = A[h, dy].reshape(4 * ROWS, HALF)
            term = lax.dot_general(left, B[h, at, :], (((1,), (1,)), ((), ())), preferred_element_type=F32)
            value = term if value is None else value + term
        for dx in range(4):
            T[dy, dx, :, at] = ratio(value[dx * ROWS:(dx + 1) * ROWS], dy, dx, 5)

    def alpha_term(h, d2):
        raw = {2: (0, 1, 2, 3), 1: (1, 3), 3: (0, 2), 0: ()}[d2]

        def one(j, carry):
            at = pl.ds(pl.multiple_of(j * 256, 256), 256)
            left = (T[d2] if h == 0 else T[:, d2]).reshape(4 * ROWS, BROWS)
            value = jnp.dot(left, B[h, :, at], preferred_element_type=F32)
            for u in range(4):
                block = value[u * ROWS:(u + 1) * ROWS]
                if u in raw:
                    S1[h, d2, u, :, at] = encode(block)
                else:
                    G[h, d2, u, :, at] = block
            return carry

        lax.fori_loop(0, 5, one, 0, unroll=True)

    def beta_term(h, low, high):
        def one(j, carry):
            at = pl.ds(pl.multiple_of(j * 256, 256), 256)
            right = A[h, :, :, :, at].reshape(BROWS, 256)
            value = jnp.dot(TT[pl.ds(low * 96, (high - low) * 96), :], right, preferred_element_type=F32)
            for p in range(low, high):
                base = (p - low) * 96
                GBO[h, p, :, at] = value[base:base + ROWS]
                GBS[h, p, :, at] = value[base + ROWS:base + 2 * ROWS]
            return carry

        lax.fori_loop(0, 5, one, 0, unroll=True)
        for p in range(low, high):
            start(("gsib", h, p))

    def by_rows(body):
        def one(step, carry):
            body(pl.ds(pl.multiple_of(step * 16, 16), 16))
            return carry

        lax.fori_loop(0, ROWS // 16, one, 0)

    for copy in local:
        copy.wait()
    pl.semaphore_wait(barrier, 7)
    H = (0, 1)
    def z_pass(k, q):
        h = q // 2
        arrived(("z+", q, k), ("z-", q, k))
        if k < 3:
            start(("z+", q, k + 1), ("z-", q, k + 1))
        else:
            start(("z4", q))
        if q % 2 == 1:
            start(("sib", h, k), ("sib", h, 8 - k))

    for h in H:
        start(("p1+", h), ("p1-", h))
    for q in range(4):
        start(("z+", q, 1), ("z-", q, 1))
    for h in H:
        start(("p2+", h, 0), ("p2-", h, 0))
    for h in H:
        start(("sib", h, 0))

    eye = lax.broadcasted_iota(jnp.int32, (ROWS, 128), 0) == lax.broadcasted_iota(jnp.int32, (ROWS, 128), 1)

    def energies(ref, column):
        return jnp.concatenate([ref[pl.ds(3 * column + i, 1), :] for i in range(3)], axis=1)

    for dx in range(4):
        row = jnp.broadcast_to(energies(virt_a, (x + dx) % 4), (8, 384))
        row = pltpu.roll(row, (384 - 96 * z_lo - 48 * core) % 384, 1)[0:1, :128]
        column = jnp.sum(jnp.where(eye, jnp.broadcast_to(row, (ROWS, 128)), 0.0), axis=1, keepdims=True)
        VA[dx] = jnp.broadcast_to(column, (ROWS, 128))
    lanes = lax.broadcasted_iota(jnp.int32, (8, BROWS), 1)
    part = energies(virt_b, x)
    ring_virt = jnp.broadcast_to(jnp.concatenate([part, part], axis=1), (8, BROWS))
    ring_occ = jnp.where(lanes < 384, occ_b[y], occ_b[4 + y])
    vb = jnp.zeros((8, BROWS), F32)
    ob = jnp.zeros((8, BROWS), F32)
    for r, p in POS.items():
        there = (z + r) % 8
        for k in range(2):
            shift = (96 * p + 768 - 96 * there + (48 * core if k else 768 - 48 * core)) % 768
            here = (lanes >= 96 * p + 48 * k) & (lanes < 96 * p + 48 * k + 48)
            vb = jnp.where(here, pltpu.roll(ring_virt, shift, 1), vb)
            ob = jnp.where(here, pltpu.roll(ring_occ, shift, 1), ob)
    vb, ob = vb[0:1], ob[0:1]

    def inverses(block, carry):
        dy, dx = block // 4, block % 4
        occ = occ_a[z_hi * 4 + (y + dy) % 4]
        for tile in range(6):
            lanes = slice(tile * 128, tile * 128 + 128)
            RD[dy, dx, :, pl.ds(tile * 128, 128)] = -1.0 / (VA[dx] + vb[:, lanes] - occ - ob[:, lanes])
        return carry

    lax.fori_loop(0, 16, inverses, 0)

    z_pass(1, 0)
    for h in H:
        arrived(("p1+", h), ("p1-", h))
        start(("p1f+", h), ("p1f-", h))
    for u in (3, 1):
        for h in H:
            start(("p2+", h, u), ("p2-", h, u))
    z_pass(1, 1)
    z_pass(1, 2)
    z_pass(1, 3)
    z_pass(2, 0)
    for h in H:
        arrived(("p1f+", h), ("p1f-", h))
        start(("p2+", h, 2), ("p2-", h, 2))
    for h in H:
        arrived(("p2+", h, 0), ("p2-", h, 0))
        start(("p2f", h, 0))
    z_pass(2, 1)
    for h in H:
        arrived(("sib", h, 0), ("sib", h, 1), ("sib", h, 7))
        integrals(h, 0, 0, 256)
    z_pass(2, 2)
    for h in H:
        arrived(("p2+", h, 3), ("p2-", h, 3))
        start(("p2f", h, 3))
    z_pass(2, 3)
    z_pass(3, 0)
    for h in H:
        arrived(("p2+", h, 1), ("p2-", h, 1))
        start(("p2f", h, 1))
    z_pass(3, 1)
    z_pass(3, 2)
    for h in H:
        arrived(("p2+", h, 2), ("p2-", h, 2))
        start(("p2f", h, 2))
    z_pass(3, 3)
    for h in H:
        integrals(h, 1, 0, 256)
        integrals(h, 3, 0, 256)
    for h in H:
        arrived(("sib", h, 2), ("sib", h, 6), ("sib", h, 3))
        for d2 in (0, 1, 3):
            integrals(h, d2, 256, 256)
    for h in H:
        arrived(("z4", 2 * h), ("z4", 2 * h + 1))
        start(("sib", h, 4))
    for h in H:
        arrived(("sib", h, 5))
        for d2 in (0, 1, 3):
            integrals(h, d2, 512, 128)
    amplitudes(9, near_place)
    for h in H:
        for u in (0, 3, 1, 2):
            arrived(("p2f", h, u))
        integrals(h, 2, 0, 256)
        integrals(h, 2, 256, 256)
        integrals(h, 2, 512, 128)
    for h in H:
        arrived(("sib", h, 4))
    for dy in range(4):
        last_amplitudes(dy)
    transpose(5)

    outward = {}

    def put(which, h):
        target = (ga_out, gb_out)[which].at[0, :, pl.ds(h * HALF, HALF)]
        outward[which, h] = pltpu.make_async_copy(OUT.at[which, h], target, out_sem.at[which, h])
        outward[which, h].start()

    def add_first(h, u):
        d2 = 1 if u % 2 == 0 else 3
        arrived(("1a", h, u))

        def body(rows):
            S1[h, d2, u, rows] = encode(G[h, d2, u, rows] + decode(R1A[h, u, rows]))

        by_rows(body)
        start(("1b+" if d2 == 1 else "1b-", h, u))

    def plane_sum(h, u, rows):
        return G[h, 0, u, rows] + decode(R1B[h, 0, u, rows]) + decode(R1B[h, 1, u, rows])

    def z_send(q, r):
        h, p, cols = q // 2, POS[r], (first, second)[q % 2]
        chained = r in (1, 2, 6, 7) or (r, h) in ((3, 0), (5, 1))
        if q % 2 == 0:
            arrived(("gsib", h, p))
        if (r, h) in ((3, 0), (5, 1)):
            arrived(("rz", q, 4))
        elif chained:
            arrived(("rz", q, r + 1 if r < 4 else r - 1))

        def body(rows):
            value = GBO[h, p, rows, cols] + GBR[h, p, rows, cols]
            if chained:
                value = value + decode(RZ[q, r, rows])
            SZ[q, r, rows] = encode(value)

        by_rows(body)
        start(("rz", q, r))

    steps = [((0, 4), (2, 4)), ((1, 4), (3, 4)), ((2, 3), (0, 5)), ((3, 3), (1, 5))]
    for r in (3, 2, 1):
        steps += [((0, r), (2, 8 - r)), ((1, r), (3, 8 - r))]
        if r > 1:
            steps += [((2, r - 1), (0, 9 - r)), ((3, r - 1), (1, 9 - r))]

    def z_step(index):
        for q, r in steps[index]:
            z_send(q, r)

    def second_far(h):
        arrived(("1b+", h, 2), ("1b-", h, 2))

        def body(rows):
            S2[h, 2, rows] = encode(plane_sum(h, 2, rows))

        by_rows(body)
        start(("2a+", h), ("2a-", h))

    def second_near(h, u):
        arrived(("1b+", h, u), ("1b-", h, u))
        arrived(("2a+" if u == 1 else "2a-", h))
        added, plain = (first, second) if u == 1 else (second, first)

        def body(rows):
            value = plane_sum(h, u, rows)
            S2[h, u, rows, plain] = encode(value[:, :QUART] if u == 3 else value[:, QUART:])
            value = value[:, QUART:] if u == 3 else value[:, :QUART]
            S2[h, u, rows, added] = encode(value + decode(R2A[h, rows, added]))

        by_rows(body)
        start(("2b+" if u == 1 else "2b-", h))

    for h in H:
        beta_term(h, 7, 8)
    amplitudes(7, far_place)
    for tile in range(5):
        transpose(tile)
    for h in H:
        alpha_term(h, 2)
        for u in (2, 1, 3, 0):
            start(("1a", h, u))
        if h == 0:
            z_step(0)
    beta_term(1, 5, 7)
    z_step(1)
    beta_term(0, 5, 7)
    for h in H:
        alpha_term(h, 3)
        start(("1b-", h, 2))
    z_step(2)
    z_step(3)
    alpha_term(0, 1)
    alpha_term(1, 1)
    z_step(4)
    beta_term(1, 3, 5)
    for h in H:
        add_first(h, 2)
        start(("1b+", h, 1))
    z_step(5)
    for h in H:
        add_first(h, 1)
    beta_term(0, 3, 5)
    z_step(6)
    for h in H:
        start(("1b+", h, 3))
        add_first(h, 3)
    z_step(7)
    for h in H:
        alpha_term(h, 0)
    beta_term(1, 1, 3)
    z_step(8)
    beta_term(0, 1, 3)
    for h in H:
        second_far(h)
    for h in H:
        start(("1b-", h, 0))
        add_first(h, 0)
    z_step(9)
    z_step(10)
    for h in H:
        beta_term(h, 0, 1)
    z_step(11)
    z_step(12)
    z_step(13)
    for h in H:
        second_near(h, 1)
        second_near(h, 3)
    for h in H:
        arrived(("1b+", h, 0), ("1b-", h, 0))

        def body(rows):
            G[h, 0, 0, rows] = plane_sum(h, 0, rows)

        by_rows(body)
    for h in H:
        arrived(("gsib", h, 0))
        for q in (2 * h, 2 * h + 1):
            arrived(("rz", q, 1), ("rz", q, 7))

        def body(rows):
            for part, cols in enumerate((first, second)):
                q = 2 * h + part
                OUT[1, h, rows, cols] = (
                    GBO[h, 0, rows, cols] + GBR[h, 0, rows, cols] + decode(RZ0[q, 0, rows]) + decode(RZ0[q, 1, rows])
                )

        by_rows(body)
        put(1, h)
    for h in H:
        arrived(("2b+", h), ("2b-", h))

        def body(rows):
            OUT[0, h, rows] = (
                G[h, 0, 0, rows] + decode(R2B[h, 0, rows]) + decode(R2B[h, 1, rows])
            )

        by_rows(body)
        put(0, h)
    for copy in list(outward.values()):
        copy.wait()
    for copy in copies.values():
        copy.wait_send()


def hand_over(ga_in, gb_in, ga_out, gb_out, held, in_sem, out_sem):
    pairs = [(w, h) for h in range(2) for w in range(2)]
    source, target = (ga_in, gb_in), (ga_out, gb_out)
    inward = [
        pltpu.make_async_copy(source[w].at[0, :, pl.ds(h * HALF, HALF)], held.at[w, h], in_sem.at[w, h])
        for w, h in pairs
    ]
    outward = [
        pltpu.make_async_copy(held.at[w, h], target[w].at[0, :, pl.ds(h * HALF, HALF)], out_sem.at[w, h])
        for w, h in pairs
    ]
    for copy in inward:
        copy.start()
    for before, after in zip(inward, outward):
        before.wait()
        after.start()
    for copy in outward:
        copy.wait()


def body(orbital_alpha, orbital_beta, occ_alpha, occ_beta, virt_alpha, virt_beta):
    block = (ROWS, HALF)
    smem = pl.BlockSpec(memory_space=pltpu.SMEM)
    vmem = pl.BlockSpec(memory_space=pltpu.VMEM)
    hbm = pl.BlockSpec(memory_space=pl.ANY)
    out = jax.ShapeDtypeStruct((1, ROWS, 2 * HALF), F32)
    count = 160
    sums = pl.pallas_call(
        kernel,
        out_shape=(out, out),
        in_specs=[smem, smem, vmem, vmem, hbm, hbm],
        out_specs=(hbm, hbm),
        scratch_shapes=[
            pltpu.VMEM((2, 4, 4) + block, BF16),
            pltpu.VMEM((2, BROWS, HALF), BF16),
            pltpu.VMEM((2, 4, 4, ROWS, BROWS), F32),
            pltpu.VMEM((4, 4, ROWS, BROWS), BF16),
            pltpu.VMEM((BROWS, BROWS), BF16),
            pltpu.VMEM((2, 4, 4) + block, F32),
            pltpu.VMEM((2, 8) + block, F32),
            pltpu.VMEM((2, 8) + block, F32),
            pltpu.VMEM((2, 8) + block, F32),
            pltpu.VMEM((2, 4, 4) + block, BF16),
            pltpu.VMEM((2, 4) + block, BF16),
            pltpu.VMEM((2, 2, 4) + block, BF16),
            pltpu.VMEM((2, 4) + block, BF16),
            pltpu.VMEM((2,) + block, BF16),
            pltpu.VMEM((2, 2) + block, BF16),
            pltpu.VMEM((4, 8, ROWS, QUART), BF16),
            pltpu.VMEM((4, 8, ROWS, QUART), BF16),
            pltpu.VMEM((4, 2, ROWS, QUART), BF16),
            pltpu.VMEM((4, ROWS, 128), F32),
            pltpu.VMEM((4, 4, ROWS, BROWS), F32),
            pltpu.VMEM((2, 2) + block, F32),
            pltpu.SemaphoreType.DMA((2, 2)),
            pltpu.SemaphoreType.DMA((4,)),
            pltpu.SemaphoreType.DMA((count,)),
            pltpu.SemaphoreType.DMA((count,)),
        ],
        compiler_params=pltpu.CompilerParams(
            collective_id=0, has_side_effects=True, vmem_limit_bytes=66 * 1000 * 1000
        ),
    )(occ_alpha, occ_beta, virt_alpha.reshape(12, 128), virt_beta.reshape(12, 128), orbital_alpha, orbital_beta)
    return pl.pallas_call(
        hand_over,
        out_shape=(out, out),
        in_specs=[hbm, hbm],
        out_specs=(hbm, hbm),
        scratch_shapes=[
            pltpu.VMEM((2, 2) + block, F32),
            pltpu.SemaphoreType.DMA((2, 2)),
            pltpu.SemaphoreType.DMA((2, 2)),
        ],
        compiler_params=pltpu.CompilerParams(vmem_limit_bytes=66 * 1000 * 1000),
    )(*sums)


def solution(mesh):
    in_specs = (P("grp", "slab", None), P("grp", "slab", None), P(), P(), P(), P())
    out_specs = (P("grp", "slab", None), P("grp", "slab", None))
    return jax.shard_map(body, mesh=mesh, in_specs=in_specs, out_specs=out_specs, check_vma=False)
```
